32 devices in a mesh: group: 4 (over z), member: 8 (over y, x, core).
Axes of the slice: x: 2, y: 2, z: 4, core: 2. Of those that a mesh axis runs over, the one named last changes fastest.
Arguments:
- embeddings: bfloat16 [24576, 1024], P(('group', 'member')), may hold values from -18 to 18
- prior: float32 [24576, 1000], P(('group', 'member')), may hold values from 0.05 to 5
- source_member: int32 [4, 8, 4], P('group'), may hold values from 0 to 7, as said below
- source_block: int32 [4, 8, 4], P('group'), may hold values from 0 to 5
- cross_block: int32 [4, 8, 2], P(None, 'member'), may hold values from 0 to 5
- row_links: int32 [24576, 4], P(('group', 'member')), may hold values from 0 to 5
Outputs:
- propagated: float32 [24576, 1000], P(('group', 'member'))
The draws below stay inside these ranges and needn't reach their ends.
Inputs may be any that keep to these rules, and one draw needn't show every extreme that they name: `source_member`: no device names itself, and the members in one device's list are distinct. Over all lists of one group no member is named more than 7 times, and in every group some member is named exactly 7 times.
All inputs are finite; a program needn't handle non-finite values.
Results may differ from the reference program's by a relative error of at most 0.0079.
Values may be sent and summed in bfloat16 or wider, within the bound.
A program may use at most 64 MiB of HBM per device.

```python
import math
import jax
import jax.numpy as jnp
from jax import lax

D = 1024
C = 1000
ROWS_DEV = 768
BR = 128
IN_SLOTS = 4
CROSS = 2
SERVE_CAP = 7
LINKS = 4
ITERS = 2
BLOCKS_DEV = 6
SLOTS = 6
TOTAL = 24576
N_GROUP = 4
N_MEMBER = 8


def link_table(key):
    return jax.random.randint(jax.random.fold_in(key, 31), (TOTAL, LINKS), 0, SLOTS).astype(jnp.int32)


def draw_row_links(key, part):
    return link_table(key)


def draw_embeddings(key, part):
    return jnp.clip(jax.random.normal(key, (TOTAL, D), jnp.float32), -6.0, 6.0).astype(jnp.bfloat16)


def arranged(subkey):
    order = jax.random.permutation(subkey, N_MEMBER).astype(jnp.int32)
    positions = jnp.arange(N_MEMBER, dtype=jnp.int32)
    offsets = jnp.arange(1, IN_SLOTS + 1, dtype=jnp.int32)
    at_position = order[(positions[:, None] + offsets[None, :]) % N_MEMBER]
    redirect = (positions[:, None] >= 1) & (positions[:, None] <= SERVE_CAP - IN_SLOTS) & (offsets[None, :] == 1)
    at_position = jnp.where(redirect, order[0], at_position)
    return jnp.zeros((N_MEMBER, IN_SLOTS), jnp.int32).at[order].set(at_position)


def draw_source_member(key, part):
    subkeys = jax.random.split(jax.random.fold_in(key, 21), N_GROUP)
    return jax.vmap(arranged)(subkeys).astype(jnp.int32)


def place_ends(values, stream_key, smallest, largest):
    extent = values.shape
    place = [jax.random.randint(jax.random.fold_in(stream_key, axis), (), 0, extent[axis]) for axis in range(len(extent))]
    values = values.at[tuple(place)].set(smallest)
    longest = extent.index(max(extent))
    place[longest] = (place[longest] + 1) % extent[longest]
    return values.at[tuple(place)].set(largest)


def steps_of(rng, dims, cuts, least, largest):
    factor_of = 1.0
    for axis_at, blocks in cuts:
        draws = jax.random.uniform(jax.random.fold_in(jax.random.fold_in(rng, 6), axis_at), (blocks,), jnp.float32, least / len(cuts), largest / len(cuts))
        factor_of = factor_of * jnp.repeat(jnp.exp(draws), dims[axis_at] // blocks).reshape((-1,) + (1,) * (len(dims) - 1 - axis_at))
    return factor_of


def setup_inputs(seed: int = 0) -> dict:
    streams_of = jax.random.split(jax.random.key(seed), 7)
    return {
        "embeddings": draw_embeddings(jax.random.fold_in(streams_of[6], 71), 0),
        "prior": jnp.clip(jnp.exp(math.log(5.0) - 4.6051702 * jax.random.uniform(streams_of[1], (TOTAL, C), jnp.float32) ** steps_of(streams_of[1], (TOTAL, C), ((0, 32),), -0.2, 0.2)), 0.05, 5.0),
        "source_member": draw_source_member(jax.random.fold_in(streams_of[6], 71), 0),
        "source_block": place_ends(jax.random.randint(streams_of[3], (N_GROUP, N_MEMBER, IN_SLOTS), 0, BLOCKS_DEV), jax.random.fold_in(streams_of[3], 1), 0, BLOCKS_DEV - 1).astype(jnp.int32),
        "cross_block": place_ends(jax.random.randint(streams_of[4], (N_GROUP, N_MEMBER, CROSS), 0, BLOCKS_DEV), jax.random.fold_in(streams_of[4], 1), 0, BLOCKS_DEV - 1).astype(jnp.int32),
        "row_links": draw_row_links(jax.random.fold_in(streams_of[6], 71), 0),
    }


MIXING = 0.8


def allowed_mask(row_links):
    slot_ids = jnp.arange(SLOTS, dtype=jnp.int32)
    slot_hits = jnp.any(row_links[:, :, None] == slot_ids[None, None, :], axis=1)
    neighbour_mask = jnp.repeat(slot_hits, BR, axis=1)
    local_mask = jnp.logical_not(jnp.eye(ROWS_DEV, dtype=bool))
    return jnp.concatenate([local_mask, neighbour_mask], axis=1)


def kernel_weights(queries, key_rows, allowed):
    scores = jnp.dot(queries, key_rows.T, preferred_element_type=jnp.float32) * (D ** -0.5)
    scores = jnp.where(allowed, scores, -jnp.inf)
    highest = jnp.max(scores, axis=1, keepdims=True)
    powers = jnp.where(allowed, jnp.exp(scores - highest), 0.0)
    return (powers / jnp.sum(powers, axis=1, keepdims=True)).astype(jnp.bfloat16)


def sharpen(weights, key_labels, prior_share):
    mixed = MIXING * jnp.dot(weights, key_labels, preferred_element_type=jnp.float32) + (1.0 - MIXING) * prior_share
    squared = mixed * mixed
    return squared / jnp.sum(squared, axis=1, keepdims=True)


def collect(blocks_all, device, members, block_ids, cross_ids):
    group_index = device // N_MEMBER
    member_index = device % N_MEMBER
    inner = blocks_all[group_index * N_MEMBER + members, block_ids]
    below_device = ((group_index + N_GROUP - 1) % N_GROUP) * N_MEMBER + member_index
    above_device = ((group_index + 1) % N_GROUP) * N_MEMBER + member_index
    outer = blocks_all[jnp.stack([below_device, above_device]).astype(jnp.int32), cross_ids]
    lane_count = blocks_all.shape[-1]
    return jnp.concatenate([inner.reshape(-1, lane_count), outer.reshape(-1, lane_count)], axis=0)


def reference(embeddings, prior, source_member, source_block, cross_block, row_links):
    devices = N_GROUP * N_MEMBER
    emb_blocks = embeddings.reshape(devices, ROWS_DEV // BR, BR, D)
    prior_share = prior / jnp.sum(prior, axis=1, keepdims=True)
    labels = prior_share.astype(jnp.bfloat16)
    device_ids = jnp.arange(devices, dtype=jnp.int32)
    emb_dev = embeddings.reshape(devices, ROWS_DEV, D)
    share_dev = prior_share.reshape(devices, ROWS_DEV, C)
    links_dev = row_links.reshape(devices, ROWS_DEV, LINKS)
    members_dev = source_member.reshape(devices, IN_SLOTS)
    blocks_dev = source_block.reshape(devices, IN_SLOTS)
    cross_dev = cross_block.reshape(devices, CROSS)
    result = prior_share
    for iteration in range(ITERS):
        lab_blocks = labels.reshape(devices, ROWS_DEV // BR, BR, C)
        lab_dev = labels.reshape(devices, ROWS_DEV, C)

        def one_device(items):
            device, queries, own_labels, share_rows, links, members, block_ids, cross_ids = items
            key_rows = jnp.concatenate([queries, collect(emb_blocks, device, members, block_ids, cross_ids)], axis=0)
            key_labels = jnp.concatenate([own_labels, collect(lab_blocks, device, members, block_ids, cross_ids)], axis=0)
            weights = kernel_weights(queries, key_rows, allowed_mask(links))
            return sharpen(weights, key_labels, share_rows)

        result = lax.map(one_device, (device_ids, emb_dev, lab_dev, share_dev, links_dev, members_dev, blocks_dev, cross_dev))
        result = result.reshape(devices * ROWS_DEV, C)
        labels = result.astype(jnp.bfloat16)
    return result * C
```

```python
import functools

import jax
import jax.numpy as jnp
from jax import lax
from jax.experimental import pallas as pl
from jax.experimental.pallas import tpu as pltpu
from jax.sharding import PartitionSpec as P

BR = 128
SERVE_CAP = 7
ITERS = 2


MIXING = 0.8


def extended(value, sides, width):
    for axis, dim in sides:
        size, length = (lax.axis_size(axis), value.shape[dim])
        up = [(i, (i + 1) % size) for i in range(size)]
        down = [(j, i) for i, j in up]
        last = lax.slice_in_dim(value, length - width, length, axis=dim)
        first = lax.slice_in_dim(value, 0, width, axis=dim)
        before = lax.ppermute(last, axis, up)
        after = lax.ppermute(first, axis, down)
        value = jnp.concatenate([before, value, after], axis=dim)
    return value


def allowed_mask(row_links, near_total, slot_total, row_count, block_rows):
    slot_ids = jnp.arange(slot_total, dtype=jnp.int32)
    slot_hits = jnp.any(row_links[:, :, None] == slot_ids[None, None, :], axis=1)
    near_mask = jnp.tile(slot_hits[:, :near_total], (1, block_rows))
    far_mask = jnp.repeat(slot_hits[:, near_total:], block_rows, axis=1)
    row_ids = lax.broadcasted_iota(jnp.int32, (row_count, row_count), 0)
    col_ids = lax.broadcasted_iota(jnp.int32, (row_count, row_count), 1)
    local_mask = row_ids != col_ids
    return jnp.concatenate([local_mask, near_mask, far_mask], axis=1)


def kernel_weights(queries, key_rows, allowed):
    features = queries.shape[1]
    scores = lax.dot_general(
        queries, key_rows, (((1,), (1,)), ((), ())), preferred_element_type=jnp.float32
    )
    scores = scores * features ** (-0.5)
    scores = jnp.where(allowed, scores, -jnp.inf)
    highest = jnp.max(scores, axis=1, keepdims=True)
    powers = jnp.where(allowed, jnp.exp(scores - highest), 0.0)
    return (powers / jnp.sum(powers, axis=1, keepdims=True)).astype(jnp.bfloat16)


def sharpen(weights, key_labels, prior_share):
    mixed = (
        MIXING * jnp.dot(weights, key_labels, preferred_element_type=jnp.float32)
        + (1.0 - MIXING) * prior_share
    )
    squared = mixed * mixed
    return squared / jnp.sum(squared, axis=1, keepdims=True)


def one_hot(ids, count):
    return (ids[..., None] == jnp.arange(count, dtype=jnp.int32)).astype(jnp.bfloat16)


def near_keys(delivered):
    return delivered.reshape(-1, delivered.shape[-1])


def far_keys(padded):
    return jnp.concatenate([padded[0], padded[-1]], axis=0)


def relay_body(embeddings, prior, source_member, source_block, cross_block, row_links):
    member_count = lax.axis_size("member")
    group_count = lax.axis_size("group")
    group_index = lax.axis_index("group")
    member_index = lax.axis_index("member")
    row_count, features = embeddings.shape
    classes = prior.shape[1]
    block_rows = BR
    block_count = row_count // block_rows
    piece_rows = block_rows // member_count
    owners = source_member[0]
    slot_count = owners.shape[1]
    flat_owner = owners.reshape(-1)
    flat_block = source_block[0].reshape(-1)
    order_ids = jnp.arange(flat_owner.shape[0], dtype=jnp.int32)
    earlier = (flat_owner[:, None] == flat_owner[None, :]) & (
        order_ids[None, :] < order_ids[:, None]
    )
    rank_ids = jnp.sum(earlier.astype(jnp.int32), axis=1)
    serve_ids = jnp.arange(SERVE_CAP, dtype=jnp.int32)
    serving = (flat_owner[None, :] == member_index) & (rank_ids[None, :] == serve_ids[:, None])
    served_blocks = jnp.sum(jnp.where(serving, flat_block[None, :], 0), axis=1)
    served_hot = one_hot(served_blocks, block_count)
    rank_grid = rank_ids.reshape(member_count, slot_count)
    deliver_hot = one_hot(owners, member_count)[..., :, None] * one_hot(rank_grid, SERVE_CAP)[..., None, :]
    below_group = (group_index + group_count - 1) % group_count
    above_group = (group_index + 1) % group_count
    group_ids = jnp.arange(group_count, dtype=jnp.int32)
    cross_pick = jnp.stack([
        jnp.sum(jnp.where(group_ids == below_group, cross_block[:, 0, 1], 0)),
        jnp.sum(jnp.where(group_ids == above_group, cross_block[:, 0, 0], 0)),
    ])
    cross_hot = one_hot(cross_pick, block_count)
    allowed = allowed_mask(
        row_links, slot_count, slot_count + cross_block.shape[2], row_count, block_rows
    )
    prior_share = prior / jnp.sum(prior, axis=1, keepdims=True)
    labels = prior_share.astype(jnp.bfloat16)
    emb_blocks = embeddings.reshape(block_count, block_rows, features)

    def cross_of(blocks):
        return jnp.einsum("cb,brl->crl", cross_hot, blocks, preferred_element_type=jnp.float32).astype(jnp.bfloat16)

    def relay_pieces(flat_rows):
        blocks = flat_rows.reshape(block_count, member_count, piece_rows, flat_rows.shape[-1])
        return jnp.einsum("sb,bmpl->mpsl", served_hot, blocks, preferred_element_type=jnp.float32).astype(jnp.bfloat16)

    def deliver_pieces(received):
        return jnp.einsum("mkos,opsl->mpkl", deliver_hot, received, preferred_element_type=jnp.float32).astype(jnp.bfloat16)

    result = prior_share
    emb_relay = lax.all_to_all(
        relay_pieces(embeddings), "member", split_axis=0, concat_axis=0, tiled=True
    )
    emb_near = lax.all_to_all(
        deliver_pieces(emb_relay), "member", split_axis=0, concat_axis=0, tiled=True
    )
    emb_far = extended(cross_of(emb_blocks), (("group", 0),), 1)
    key_rows = jnp.concatenate([embeddings, near_keys(emb_near), far_keys(emb_far)], axis=0)
    weights = kernel_weights(embeddings, key_rows, allowed)
    for iteration in range(ITERS):
        lab_blocks = labels.reshape(block_count, block_rows, classes)
        lab_relay = lax.all_to_all(
            relay_pieces(labels), "member", split_axis=0, concat_axis=0, tiled=True
        )
        lab_near = lax.all_to_all(
            deliver_pieces(lab_relay), "member", split_axis=0, concat_axis=0, tiled=True
        )
        lab_far = extended(cross_of(lab_blocks), (("group", 0),), 1)
        key_labels = jnp.concatenate([labels, near_keys(lab_near), far_keys(lab_far)], axis=0)
        result = sharpen(weights, key_labels, prior_share)
        labels = result.astype(jnp.bfloat16)
    return result * classes


MESH = pl.DeviceIdType.MESH
TABLE = 32
AT_CODES, AT_RELAYS, AT_PLACE, AT_SUM, AT_PICK = 1, 3, 5, 9, 13
FIRST, RELAY, PURE = (0, 1), (2, 3), 4
LINKS_OUT = ((0, 1), (1, 2))


def partner_of(member, mask, member_count):
    bit = 1
    while bit < member_count:
        if mask & bit:
            member = member + bit - 2 * bit * (member // bit % 2)
        bit *= 2
    return member


def same(left, right):
    gap = left - right
    return 1 - jnp.minimum(gap * gap, 1)


def pairs_in(bits):
    return bits - (bits >> 1)


def route_kernel(group_count, block_count, owners, blocks, table, mine, others, send_sem, recv_sem):
    group = lax.axis_index("group")
    me = lax.axis_index("member")
    core = me % 2
    in_slots, members = owners.shape
    targets = [((group + i) % group_count, me) for i in range(1, group_count)]
    barrier = pltpu.get_barrier_semaphore()
    for target in targets:
        pl.semaphore_signal(barrier, inc=1, device_id=target, device_id_type=MESH)

    def named_of(p):
        bits = jnp.int32(0)
        for k in range(in_slots):
            bits += jnp.left_shift(jnp.int32(1), owners[k, p])
        return bits

    named = [named_of(p) for p in range(members)]

    def flow(src, dst):
        return sum(pairs_in((named[2 * dst + t] >> (2 * src)) & 3) for t in (0, 1))

    chips = range(members // 2)
    flat = [[flow(c, c ^ 1), flow(c, c ^ 2)] for c in chips]
    cornered = [flow(c, c ^ 3) for c in chips]
    choice = lax.broadcasted_iota(jnp.int32, (8, 128), 0) * 128 + lax.broadcasted_iota(jnp.int32, (8, 128), 1)
    choice = choice & 255
    turn = [(choice >> (2 * c)) & 3 for c in chips]
    fits = choice >= 0
    load = jnp.zeros_like(choice)
    for c in chips:
        fits &= (turn[c] <= 2) & (turn[c] <= cornered[c]) & (turn[c] >= cornered[c] - 2)
        load = jnp.maximum(load, turn[c] - turn[c ^ 2] + (flat[c][0] + cornered[c ^ 2]))
        load = jnp.maximum(load, turn[c ^ 1] - turn[c] + (flat[c][1] + cornered[c]))
    best = jnp.min(jnp.where(fits, load * 256 + choice, 1 << 20))
    need = best >> 8

    mine[...] = jnp.full(mine.shape, need, jnp.int32)
    pl.semaphore_wait(barrier, len(targets))
    copies = []
    for i, target in enumerate(targets):
        copy = pltpu.make_async_remote_copy(
            src_ref=mine, dst_ref=others.at[i], send_sem=send_sem.at[i], recv_sem=recv_sem.at[i],
            device_id=target, device_id_type=MESH,
        )
        copy.start()
        copies.append(copy)

    packed_corner = sum(cornered[c] << (4 * c) for c in chips)
    chip = [partner_of(me, 2 * e, members) // 2 for e in range(4)]
    bits = [[named_of(2 * chip[e] + t) for t in (0, 1)] for e in range(4)]

    def corner_of(c):
        return (packed_corner >> (4 * c)) & 15

    def turn_of(c):
        return (best >> (2 * c)) & 3

    def hop(e, link):
        if link == 0:
            return turn_of(chip[e]), corner_of(chip[e ^ 2]) - turn_of(chip[e ^ 2])
        return corner_of(chip[e]) - turn_of(chip[e]), turn_of(chip[e ^ 1])

    def flag(src, s, dst, t):
        return (bits[dst][t] >> (2 * chip[src] + s)) & 1

    def pick(src, dst):
        total = jnp.int32(0)
        for k in range(in_slots):
            total += same(owners[k, dst], src) * blocks[k, dst]
        return total

    def placed(at, relays):
        return jnp.minimum(at + jnp.where(at >= 2, relays, 0), 7)

    codes = [jnp.int32(0), jnp.int32(0)]

    def code_of(s, e, t):
        apart = core + s - 2 * core * s
        return pick(2 * chip[0] + s, 2 * chip[e] + t) + block_count * apart

    for link, e in LINKS_OUT:
        at, relays = hop(0, link)
        table[AT_RELAYS + link] = relays
        for t in (0, 1):
            for s in (0, 1):
                there = flag(0, s, e, t)
                codes[link] += there * jnp.left_shift(code_of(s, e, t), 4 * placed(at, relays))
                at += there
    at = jnp.int32(0)
    for t in (0, 1):
        for s in (0, 1):
            there = flag(0, s, 3, t)
            code = code_of(s, 3, t)
            split = turn_of(chip[0])
            early = jnp.where(at < split, there, 0)
            codes[0] += early * jnp.left_shift(code, 4 * jnp.minimum(at, 7))
            codes[1] += (there - early) * jnp.left_shift(code, 4 * jnp.maximum(at - split, 0))
            at += there
    for link in (0, 1):
        table[AT_CODES + link] = codes[link]

    wanted = [owners[k, me] for k in range(in_slots)]
    places = [same(q, partner_of(me, 1, members)) * 16 for q in wanted]
    for e in (1, 2, 3):
        flags = [[flag(e, s, 0, t) for s in (0, 1)] for t in (0, 1)]
        for s in (0, 1):
            ahead = core * (flags[0][0] + flags[0][1])
            if s == 1:
                ahead += jnp.where(core == 0, flags[0][0], flags[1][0])
            if e < 3:
                link = e - 1
                begin, relays = hop(e, link)
                place = 8 * link + placed(begin + ahead, relays)
            else:
                split = turn_of(chip[3])
                place = jnp.where(ahead < split, 8 + RELAY[0] + ahead, RELAY[0] + ahead - split)
            for k in range(in_slots):
                places[k] += same(wanted[k], 2 * chip[e] + s) * place
    for k in range(in_slots):
        table[AT_PLACE + k] = places[k]
        index = jnp.int32(0)
        for mask in range(1, members):
            index += same(wanted[k], partner_of(me, mask, members)) * (mask + 1)
        table[AT_SUM + k] = index
    for mask in range(1, members):
        table[AT_PICK + mask - 1] = pick(me, partner_of(me, mask, members))
    for i in range(AT_PICK + members - 1, TABLE):
        table[i] = jnp.int32(0)

    most = mine[...]
    for i, copy in enumerate(copies):
        copy.wait()
        most = jnp.maximum(most, others[i])
    table[0] = jnp.max(most)


def route(owners, blocks, group_count, block_count):
    smem = pl.BlockSpec(memory_space=pltpu.SMEM)
    others = max(group_count - 1, 1)
    return pl.pallas_call(
        functools.partial(route_kernel, group_count, block_count),
        out_shape=jax.ShapeDtypeStruct((TABLE,), jnp.int32),
        in_specs=[smem] * 2,
        out_specs=smem,
        scratch_shapes=[
            pltpu.VMEM((8, 128), jnp.int32),
            pltpu.VMEM((others, 8, 128), jnp.int32),
            pltpu.SemaphoreType.DMA((others,)),
            pltpu.SemaphoreType.DMA((others,)),
        ],
        compiler_params=pltpu.CompilerParams(collective_id=0, has_side_effects=True),
    )(owners, blocks)


def halves_of(classes):
    half = -(-classes // 16) * 8
    low = -(-half // 32) * 16
    return half, (low, half - low)


def spread_kernel(
    cap, member_count, group_count,
    table, cross, emb_hbm, prior_hbm, links_hbm, out, row_sums,
    share, links, scores, weights, mix, sums, sum_send, sum_recv,
    own_low, own_high, keys_low, keys_high, *rest,
):
    unit_refs, (load_sem, ex_sem, slot_sem, fwd_sem, near_sem, far_sem, sum_sem) = rest[:-7], rest[-7:]
    group = lax.axis_index("group")
    me = lax.axis_index("member")
    core = me % 2
    sibling = (group, partner_of(me, 1, member_count))
    nexts = [(group, partner_of(me, 2, member_count)), (group, partner_of(me, 4, member_count))]
    ends = [((group + 1) % group_count, me), ((group + group_count - 1) % group_count, me)]
    partners = [(group, partner_of(me, mask, member_count)) for mask in range(1, member_count)]
    everyone = ends + partners
    _, half, rows = share.shape
    classes = out.shape[0]
    block_count = rows // BR
    heights = (own_low.shape[1], own_high.shape[1])
    bands = (slice(0, heights[0]), slice(heights[0], half))
    twice = 2 * half - classes
    owns, keys = (own_low, own_high), (keys_low, keys_high)
    width = 2 * BR if block_count % 2 == 0 else BR
    in_chunk = width // BR
    chunks = rows // width
    near_at = rows + 2 * BR
    near = 4
    offsets = [(classes - half) * core, (classes - half) * (1 - core)]
    order = FIRST + tuple(range(PURE, cap))
    slots = tuple((link, s) for s in range(cap) for link in (0, 1))

    started = {}

    class Copy:
        def __init__(self, src, dst, sems, at, device):
            self.key = (id(sems), at)
            self.copy = pltpu.make_async_remote_copy(
                src_ref=src, dst_ref=dst, send_sem=sems.at[(0,) + at], recv_sem=sems.at[(1,) + at],
                device_id=device, device_id_type=MESH,
            )

        def start(self):
            started[self.key] = self
            self.copy.start()

        def wait_recv(self):
            self.copy.wait_recv()

        def wait_send(self):
            self.copy.wait_send()

    class Unit:
        def __init__(self, index, refs):
            self.index = index
            self.mine, self.oth, self.theirs, self.send, self.recv, self.fwd, self.near, self.far, self.far_in = refs

        def ex(self):
            return Copy(self.oth, self.theirs, ex_sem, (self.index,), sibling)

        def slot(self, link, s):
            i = link * cap + s
            return Copy(self.send.at[i], self.recv.at[i], slot_sem, (self.index, i), nexts[link])

        def forward(self, link, s):
            i = link * cap + s
            return Copy(self.recv.at[i], self.fwd.at[i], fwd_sem, (self.index, i), sibling)

        def sib(self, part):
            dst = self.recv if part == 1 else self.fwd
            return Copy(self.near.at[part], dst.at[2 * cap], near_sem, (self.index, part), sibling)

        def cross(self, i):
            return Copy(self.far.at[i], self.far_in.at[i], far_sem, (self.index, i), ends[i])

        def block_of(self, code):
            own = self.mine[jnp.minimum(code, block_count - 1)]
            return jnp.where(code < block_count, own, self.theirs[jnp.maximum(code - block_count, 0)])

    units = [Unit(i, unit_refs[9 * i:9 * i + 9]) for i in range(1 + 2 * ITERS)]
    emb = units[0]
    labels = [units[1 + 2 * stage:3 + 2 * stage] for stage in range(ITERS)]

    loads = [
        pltpu.make_async_copy(
            emb_hbm.at[:, :, pl.ds(pl.multiple_of(core * emb.oth.shape[2], 128), emb.oth.shape[2])],
            emb.mine, load_sem.at[0],
        ),
        pltpu.make_async_copy(
            emb_hbm.at[:, :, pl.ds(pl.multiple_of((1 - core) * emb.oth.shape[2], 128), emb.oth.shape[2])],
            emb.oth, load_sem.at[1],
        ),
        pltpu.make_async_copy(
            prior_hbm.at[pl.ds(pl.multiple_of(offsets[0], 8), half)], share.at[0], load_sem.at[2]
        ),
        pltpu.make_async_copy(
            prior_hbm.at[pl.ds(pl.multiple_of(offsets[1], 8), half)], share.at[1], load_sem.at[3]
        ),
        pltpu.make_async_copy(links_hbm, links, load_sem.at[4]),
    ]
    for copy in loads:
        copy.start()
    barrier = pltpu.get_barrier_semaphore()
    for target in everyone:
        pl.semaphore_signal(barrier, inc=1, device_id=target, device_id_type=MESH)

    codes = [[(table[AT_CODES + link] >> (4 * s)) & 15 for s in range(cap)] for link in (0, 1)]
    relays = [table[AT_RELAYS + link] for link in (0, 1)]
    places = []
    for k in range(near):
        place = table[AT_PLACE + k]
        places.append(jnp.minimum(place % 8 + cap * (place // 8), 2 * cap))
    picks = [cross[0, ends[0][0]], cross[1, ends[1][0]]]
    picks += [table[AT_PICK + i] for i in range(member_count - 1)]
    sum_at = [table[AT_SUM + k] for k in range(near)]

    def side(unit):
        for part, ref in ((0, unit.mine), (1, unit.oth)):
            unit.near[part] = ref[picks[2]]
            unit.sib(part).start()
        for i in (0, 1):
            unit.far[i, 0] = unit.mine[picks[i]]
            unit.far[i, 1] = unit.oth[picks[i]]
            unit.cross(i).start()

    def first(unit):
        unit.ex().wait_recv()
        for s in order:
            for link in (0, 1):
                unit.send[link * cap + s] = unit.block_of(codes[link][s])
                unit.slot(link, s).start()

    def relay(unit):
        for s in FIRST:
            for link in (0, 1):
                unit.slot(link, s).wait_recv()
        for s in FIRST:
            for link in (0, 1):
                passing = unit.recv[(1 - link) * cap + s]
                unit.send[link * cap + RELAY[s]] = jnp.where(
                    s < relays[link], passing, unit.block_of(codes[link][RELAY[s]])
                )
                unit.slot(link, RELAY[s]).start()
        for s in FIRST:
            for link in (0, 1):
                unit.forward(link, s).start()

    def pass_on(unit, which):
        for s in which:
            for link in (0, 1):
                unit.slot(link, s).wait_recv()
                unit.forward(link, s).start()

    pure = tuple(range(PURE, cap))

    def gathered(unit):
        for link, s in slots:
            unit.forward(link, s).wait_recv()
        for part in (0, 1):
            unit.sib(part).wait_recv()

    loads[0].wait()
    loads[1].wait()
    pl.semaphore_wait(barrier, len(everyone))
    emb.ex().start()
    loads[2].wait()
    loads[3].wait()
    first(emb)
    side(emb)

    def lanes_of(c):
        return pl.ds(pl.multiple_of(c * width, width), width)

    def summed(value, part, t):
        if part == 0 or twice == 0:
            return jnp.sum(value, axis=0, keepdims=True)
        if t == 0:
            rest, again, count = value[twice:], value[:twice], core
        else:
            rest, again, count = value[:-twice], value[-twice:], 1 - core
        total = jnp.sum(rest, axis=0, keepdims=True)
        return total + jnp.sum(again, axis=0, keepdims=True) * count.astype(jnp.float32)

    def put_blocks(stage, part, t, c, value):
        unit = labels[stage][t]
        ref = unit.oth if part else unit.mine
        for b in range(in_chunk):
            ref[c * in_chunk + b] = value[:, b * BR:(b + 1) * BR]

    def first_labels(c, _):
        lanes = lanes_of(c)
        total = jnp.zeros((1, width), jnp.float32)
        for part in (0, 1):
            for t in (0, 1):
                total += summed(share[part, bands[t], lanes], part, t)
        scale = 1.0 / total
        for part in (0, 1):
            for t in (0, 1):
                value = share[part, bands[t], lanes] * scale
                share[part, bands[t], lanes] = value
                value = value.astype(jnp.bfloat16)
                owns[t][part, :, lanes] = value
                put_blocks(0, part, t, c, value)
        return _

    lax.fori_loop(0, chunks, first_labels, 0)
    for t in (0, 1):
        labels[0][t].ex().start()
        side(labels[0][t])

    features = 2 * emb.oth.shape[2]

    def score_of(low, high):
        def against(keys, ref):
            return lax.dot_general(
                keys, ref.reshape(rows, features // 2), (((1,), (1,)), ((), ())), preferred_element_type=jnp.float32
            )

        return (against(low, emb.mine[...]) + against(high, emb.oth[...])) * features ** (-0.5)

    def own_scores(b, _):
        span = pl.ds(pl.multiple_of(b * BR, BR), BR)
        value = score_of(emb.mine[b], emb.oth[b])
        key_ids = lax.broadcasted_iota(jnp.int32, (BR, rows), 0) + b * BR
        row_ids = lax.broadcasted_iota(jnp.int32, (BR, rows), 1)
        scores[span, :] = jnp.where(key_ids != row_ids, value, -jnp.inf)
        return _

    lax.fori_loop(0, block_count, own_scores, 0)
    loads[4].wait()

    def bias_of(name):
        return jnp.max(jnp.where(links[...] == name, 0.0, -jnp.inf), axis=0, keepdims=True)

    relay(emb)
    pass_on(emb, pure)
    first(labels[0][0])
    for i in (0, 1):
        emb.cross(i).wait_recv()
        at = rows + i * BR
        scores[at:at + BR, :] = score_of(emb.far_in[i, 0], emb.far_in[i, 1]) + bias_of(near + i)
    pass_on(emb, RELAY)
    gathered(emb)
    for k in range(near):
        at = near_at + k * BR
        scores[at:at + BR, :] = score_of(emb.recv[places[k]], emb.fwd[places[k]]) + bias_of(k)
    relay(labels[0][0])

    def soften(b, _):
        lanes = pl.ds(pl.multiple_of(b * BR, BR), BR)
        value = scores[:, lanes]
        powers = jnp.exp(value - jnp.max(value, axis=0, keepdims=True))
        total = jnp.sum(powers, axis=0, keepdims=True)
        weights[:, lanes] = (powers * (1.0 / total)).astype(jnp.bfloat16)
        return _

    lax.fori_loop(0, block_count, soften, 0)
    first(labels[0][1])

    def scaled(block, at):
        return (block.astype(jnp.float32) * (1.0 / sum_recv[at][:1])).astype(jnp.bfloat16)

    def premix(stage, t):
        unit = labels[stage][t]
        for i in (0, 1):
            unit.cross(i).wait_recv()
            for part in (0, 1):
                block = unit.far_in[i, part]
                owns[t][part, :, rows + i * BR:rows + (i + 1) * BR] = scaled(block, i) if stage else block

        def body(c, _):
            lanes = lanes_of(c)
            for part in (0, 1):
                mix[part, bands[t], lanes] = jnp.dot(
                    owns[t][part], weights[:near_at, lanes], preferred_element_type=jnp.float32
                )
            return _

        lax.fori_loop(0, chunks, body, 0)

    def neighbour_mix(stage, t, finish):
        unit = labels[stage][t]
        gathered(unit)
        for k in range(near):
            for part, ref in ((0, unit.recv), (1, unit.fwd)):
                block = ref[places[k]]
                keys[t][part, :, k * BR:(k + 1) * BR] = scaled(block, sum_at[k]) if stage else block

        def body(c, _):
            lanes = lanes_of(c)
            total_sum = jnp.zeros((1, width), jnp.float32)
            for part in (0, 1):
                total = mix[part, bands[t], lanes] + jnp.dot(
                    keys[t][part], weights[near_at:, lanes], preferred_element_type=jnp.float32
                )
                mixed = MIXING * total + (1.0 - MIXING) * share[part, bands[t], lanes]
                squared = mixed * mixed
                total_sum += summed(squared, part, t)
                finish(c, lanes, part, squared)
            for b in range(in_chunk):
                value = jnp.broadcast_to(total_sum[:, b * BR:(b + 1) * BR], (8, BR))
                at = c * in_chunk + b
                sums[at] = value if t == 0 else sums[at] + value
            return _

        lax.fori_loop(0, chunks, body, 0)

    def middle(stage, t):
        def finish(c, lanes, part, squared):
            mix[part, bands[t], lanes] = squared
            put_blocks(stage + 1, part, t, c, squared.astype(jnp.bfloat16))

        return finish

    def last(t):
        def finish(c, lanes, part, squared):
            begin = pl.multiple_of(offsets[part] + bands[t].start, 8)
            out[pl.ds(begin, heights[t]), lanes] = squared

        return finish

    def sum_copy(s):
        return Copy(sum_send.at[s], sum_recv.at[s], sum_sem, (s,), everyone[s])

    def own_labels(c, _):
        lanes = lanes_of(c)
        parts = [sums[c * in_chunk + b][:1] for b in range(in_chunk)]
        scale = 1.0 / jnp.concatenate(parts, axis=1)
        for part in (0, 1):
            for t in (0, 1):
                owns[t][part, :, lanes] = (mix[part, bands[t], lanes] * scale).astype(jnp.bfloat16)
        return _

    for stage in range(ITERS):
        final = stage == ITERS - 1
        this = labels[stage]
        premix(stage, 0)
        premix(stage, 1)
        pass_on(this[0], pure + RELAY)
        neighbour_mix(stage, 0, last(0) if final else middle(stage, 0))
        if not final:
            later = labels[stage + 1]
            later[0].ex().start()
            side(later[0])
        relay(this[1])
        if not final:
            first(later[0])
        pass_on(this[1], pure + RELAY)
        neighbour_mix(stage, 1, last(1) if final else middle(stage, 1))
        if not final:
            for s in range(len(everyone)):
                sum_send[s] = sums[picks[s]]
                sum_copy(s).start()
            later[1].ex().start()
            side(later[1])
            lax.fori_loop(0, chunks, own_labels, 0)
            for s in range(len(everyone)):
                sum_copy(s).wait_recv()
            relay(later[0])
            first(later[1])

    for b in range(block_count):
        row_sums[:, b * BR:(b + 1) * BR] = sums[b]
    for copy in started.values():
        copy.wait_send()


def spread(cap, member_count, group_count, table, cross, emb, prior, links):
    block_count, _, features = emb.shape
    classes, rows = prior.shape
    half, heights = halves_of(classes)
    any_space = pl.BlockSpec(memory_space=pl.ANY)
    smem = pl.BlockSpec(memory_space=pltpu.SMEM)
    vmem = pl.BlockSpec(memory_space=pltpu.VMEM)
    bf16, f32 = jnp.bfloat16, jnp.float32
    keys = rows + 6 * BR
    partners = member_count + 1

    def unit(height, wide):
        counts = (
            (block_count,), (block_count,), (block_count,), (2 * cap,), (2 * cap + 1,), (2 * cap + 1,), (2,), (2, 2), (2, 2)
        )
        return [pltpu.VMEM(count + (height, wide), bf16) for count in counts]

    def dma(*shape):
        return pltpu.SemaphoreType.DMA((2,) + shape)

    units = 1 + 2 * ITERS
    squared, sums = pl.pallas_call(
        functools.partial(spread_kernel, cap, member_count, group_count),
        out_shape=(pltpu.VMEM((classes, rows), f32), pltpu.VMEM((8, rows), f32)),
        in_specs=[smem] * 2 + [any_space] * 3,
        out_specs=(vmem, vmem),
        scratch_shapes=[
            pltpu.VMEM((2, half, rows), f32),
            pltpu.VMEM((links.shape[0], rows), jnp.int32),
            pltpu.VMEM((keys, rows), f32),
            pltpu.VMEM((keys, rows), bf16),
            pltpu.VMEM((2, half, rows), f32),
            pltpu.VMEM((block_count, 8, BR), f32),
            pltpu.VMEM((partners, 8, BR), f32),
            pltpu.VMEM((partners, 8, BR), f32),
            pltpu.VMEM((2, heights[0], rows + 2 * BR), bf16),
            pltpu.VMEM((2, heights[1], rows + 2 * BR), bf16),
            pltpu.VMEM((2, heights[0], 4 * BR), bf16),
            pltpu.VMEM((2, heights[1], 4 * BR), bf16),
            *unit(BR, features // 2),
            *(ref for _ in range(ITERS) for height in heights for ref in unit(height, BR)),
            pltpu.SemaphoreType.DMA((5,)),
            dma(units), dma(units, 2 * cap), dma(units, 2 * cap), dma(units, 2), dma(units, 2), dma(partners),
        ],
        compiler_params=pltpu.CompilerParams(
            collective_id=cap, has_side_effects=True, vmem_limit_bytes=60 * 2**20
        ),
    )(table, cross, emb, prior, links)
    return (squared * (classes / sums[:1])).T


def spread_body(embeddings, prior, source_member, source_block, cross_block, row_links):
    member_count = lax.axis_size("member")
    group_count = lax.axis_size("group")
    rows, features = embeddings.shape
    table = route(source_member[0].T, source_block[0].T, group_count, rows // BR)
    caps = (6, 7, 8)
    branches = [functools.partial(spread, cap, member_count, group_count) for cap in caps]
    return lax.switch(
        jnp.clip(table[0] - caps[0], 0, len(caps) - 1), branches,
        table, cross_block[:, 0, :].T, embeddings.reshape(rows // BR, BR, features), prior.T, row_links.T,
    )


def solution(mesh):
    spread_fits = mesh.shape["member"] == 8
    body = spread_body if spread_fits else relay_body
    placed = (
        P(("group", "member"), None),
        P(("group", "member"), None),
        P("group", None, None),
        P("group", None, None),
        P(None, "member", None),
        P(("group", "member"), None),
    )
    return jax.shard_map(
        body, mesh=mesh, in_specs=placed, out_specs=P(("group", "member"), None), check_vma=False
    )
```

```python
import functools

import jax
import jax.numpy as jnp
from jax import lax
from jax.experimental import pallas as pl
from jax.experimental.pallas import tpu as pltpu
from jax.sharding import PartitionSpec as P

BR = 128
SERVE_CAP = 7
ITERS = 2


MIXING = 0.8


def extended(value, sides, width):
    for axis, dim in sides:
        size, length = (lax.axis_size(axis), value.shape[dim])
        up = [(i, (i + 1) % size) for i in range(size)]
        down = [(j, i) for i, j in up]
        last = lax.slice_in_dim(value, length - width, length, axis=dim)
        first = lax.slice_in_dim(value, 0, width, axis=dim)
        before = lax.ppermute(last, axis, up)
        after = lax.ppermute(first, axis, down)
        value = jnp.concatenate([before, value, after], axis=dim)
    return value


def allowed_mask(row_links, near_total, slot_total, row_count, block_rows):
    slot_ids = jnp.arange(slot_total, dtype=jnp.int32)
    slot_hits = jnp.any(row_links[:, :, None] == slot_ids[None, None, :], axis=1)
    near_mask = jnp.tile(slot_hits[:, :near_total], (1, block_rows))
    far_mask = jnp.repeat(slot_hits[:, near_total:], block_rows, axis=1)
    row_ids = lax.broadcasted_iota(jnp.int32, (row_count, row_count), 0)
    col_ids = lax.broadcasted_iota(jnp.int32, (row_count, row_count), 1)
    local_mask = row_ids != col_ids
    return jnp.concatenate([local_mask, near_mask, far_mask], axis=1)


def kernel_weights(queries, key_rows, allowed):
    features = queries.shape[1]
    scores = lax.dot_general(
        queries, key_rows, (((1,), (1,)), ((), ())), preferred_element_type=jnp.float32
    )
    scores = scores * features ** (-0.5)
    scores = jnp.where(allowed, scores, -jnp.inf)
    highest = jnp.max(scores, axis=1, keepdims=True)
    powers = jnp.where(allowed, jnp.exp(scores - highest), 0.0)
    return (powers / jnp.sum(powers, axis=1, keepdims=True)).astype(jnp.bfloat16)


def sharpen(weights, key_labels, prior_share):
    mixed = (
        MIXING * jnp.dot(weights, key_labels, preferred_element_type=jnp.float32)
        + (1.0 - MIXING) * prior_share
    )
    squared = mixed * mixed
    return squared / jnp.sum(squared, axis=1, keepdims=True)


def one_hot(ids, count):
    return (ids[..., None] == jnp.arange(count, dtype=jnp.int32)).astype(jnp.bfloat16)


def near_keys(delivered):
    return delivered.reshape(-1, delivered.shape[-1])


def far_keys(padded):
    return jnp.concatenate([padded[0], padded[-1]], axis=0)


def relay_body(embeddings, prior, source_member, source_block, cross_block, row_links):
    member_count = lax.axis_size("member")
    group_count = lax.axis_size("group")
    group_index = lax.axis_index("group")
    member_index = lax.axis_index("member")
    row_count, features = embeddings.shape
    classes = prior.shape[1]
    block_rows = BR
    block_count = row_count // block_rows
    piece_rows = block_rows // member_count
    owners = source_member[0]
    slot_count = owners.shape[1]
    flat_owner = owners.reshape(-1)
    flat_block = source_block[0].reshape(-1)
    order_ids = jnp.arange(flat_owner.shape[0], dtype=jnp.int32)
    earlier = (flat_owner[:, None] == flat_owner[None, :]) & (
        order_ids[None, :] < order_ids[:, None]
    )
    rank_ids = jnp.sum(earlier.astype(jnp.int32), axis=1)
    serve_ids = jnp.arange(SERVE_CAP, dtype=jnp.int32)
    serving = (flat_owner[None, :] == member_index) & (rank_ids[None, :] == serve_ids[:, None])
    served_blocks = jnp.sum(jnp.where(serving, flat_block[None, :], 0), axis=1)
    served_hot = one_hot(served_blocks, block_count)
    rank_grid = rank_ids.reshape(member_count, slot_count)
    deliver_hot = one_hot(owners, member_count)[..., :, None] * one_hot(rank_grid, SERVE_CAP)[..., None, :]
    below_group = (group_index + group_count - 1) % group_count
    above_group = (group_index + 1) % group_count
    group_ids = jnp.arange(group_count, dtype=jnp.int32)
    cross_pick = jnp.stack([
        jnp.sum(jnp.where(group_ids == below_group, cross_block[:, 0, 1], 0)),
        jnp.sum(jnp.where(group_ids == above_group, cross_block[:, 0, 0], 0)),
    ])
    cross_hot = one_hot(cross_pick, block_count)
    allowed = allowed_mask(
        row_links, slot_count, slot_count + cross_block.shape[2], row_count, block_rows
    )
    prior_share = prior / jnp.sum(prior, axis=1, keepdims=True)
    labels = prior_share.astype(jnp.bfloat16)
    emb_blocks = embeddings.reshape(block_count, block_rows, features)

    def cross_of(blocks):
        return jnp.einsum("cb,brl->crl", cross_hot, blocks, preferred_element_type=jnp.float32).astype(jnp.bfloat16)

    def relay_pieces(flat_rows):
        blocks = flat_rows.reshape(block_count, member_count, piece_rows, flat_rows.shape[-1])
        return jnp.einsum("sb,bmpl->mpsl", served_hot, blocks, preferred_element_type=jnp.float32).astype(jnp.bfloat16)

    def deliver_pieces(received):
        return jnp.einsum("mkos,opsl->mpkl", deliver_hot, received, preferred_element_type=jnp.float32).astype(jnp.bfloat16)

    result = prior_share
    emb_relay = lax.all_to_all(
        relay_pieces(embeddings), "member", split_axis=0, concat_axis=0, tiled=True
    )
    emb_near = lax.all_to_all(
        deliver_pieces(emb_relay), "member", split_axis=0, concat_axis=0, tiled=True
    )
    emb_far = extended(cross_of(emb_blocks), (("group", 0),), 1)
    key_rows = jnp.concatenate([embeddings, near_keys(emb_near), far_keys(emb_far)], axis=0)
    weights = kernel_weights(embeddings, key_rows, allowed)
    for iteration in range(ITERS):
        lab_blocks = labels.reshape(block_count, block_rows, classes)
        lab_relay = lax.all_to_all(
            relay_pieces(labels), "member", split_axis=0, concat_axis=0, tiled=True
        )
        lab_near = lax.all_to_all(
            deliver_pieces(lab_relay), "member", split_axis=0, concat_axis=0, tiled=True
        )
        lab_far = extended(cross_of(lab_blocks), (("group", 0),), 1)
        key_labels = jnp.concatenate([labels, near_keys(lab_near), far_keys(lab_far)], axis=0)
        result = sharpen(weights, key_labels, prior_share)
        labels = result.astype(jnp.bfloat16)
    return result * classes


MESH = pl.DeviceIdType.MESH
TABLE = 32
AT_CODES, AT_RELAYS, AT_PLACE, AT_SUM, AT_PICK = 1, 3, 5, 9, 13
FIRST, RELAY, PURE = (0, 1), (2, 3), 4
LINKS_OUT = ((0, 1), (1, 2))


def partner_of(member, mask, member_count):
    bit = 1
    while bit < member_count:
        if mask & bit:
            member = member + bit - 2 * bit * (member // bit % 2)
        bit *= 2
    return member


def same(left, right):
    gap = left - right
    return 1 - jnp.minimum(gap * gap, 1)


def pairs_in(bits):
    return bits - (bits >> 1)


def route_kernel(
    group_count, block_count, owners, blocks, emb_hbm, table, theirs, mine, others, send_sem, recv_sem, swap_sem
):
    group = lax.axis_index("group")
    me = lax.axis_index("member")
    core = me % 2
    in_slots, members = owners.shape
    targets = [((group + i) % group_count, me) for i in range(1, group_count)]
    sibling = (group, partner_of(me, 1, members))
    barrier = pltpu.get_barrier_semaphore()
    for target in targets + [sibling]:
        pl.semaphore_signal(barrier, inc=1, device_id=target, device_id_type=MESH)

    def named_of(p):
        bits = jnp.int32(0)
        for k in range(in_slots):
            bits += jnp.left_shift(jnp.int32(1), owners[k, p])
        return bits

    named = [named_of(p) for p in range(members)]

    def flow(src, dst):
        return sum(pairs_in((named[2 * dst + t] >> (2 * src)) & 3) for t in (0, 1))

    chips = range(members // 2)
    flat = [[flow(c, c ^ 1), flow(c, c ^ 2)] for c in chips]
    cornered = [flow(c, c ^ 3) for c in chips]
    choice = lax.broadcasted_iota(jnp.int32, (8, 128), 0) * 128 + lax.broadcasted_iota(jnp.int32, (8, 128), 1)
    choice = choice & 255
    turn = [(choice >> (2 * c)) & 3 for c in chips]
    fits = choice >= 0
    load = jnp.zeros_like(choice)
    for c in chips:
        fits &= (turn[c] <= 2) & (turn[c] <= cornered[c]) & (turn[c] >= cornered[c] - 2)
        load = jnp.maximum(load, turn[c] - turn[c ^ 2] + (flat[c][0] + cornered[c ^ 2]))
        load = jnp.maximum(load, turn[c ^ 1] - turn[c] + (flat[c][1] + cornered[c]))
    best = jnp.min(jnp.where(fits, load * 256 + choice, 1 << 20))
    need = best >> 8

    mine[...] = jnp.full(mine.shape, need, jnp.int32)
    pl.semaphore_wait(barrier, len(targets) + 1)
    copies = []
    for i, target in enumerate(targets):
        copy = pltpu.make_async_remote_copy(
            src_ref=mine, dst_ref=others.at[i], send_sem=send_sem.at[i], recv_sem=recv_sem.at[i],
            device_id=target, device_id_type=MESH,
        )
        copy.start()
        copies.append(copy)

    half = theirs.shape[2]
    swap = pltpu.make_async_remote_copy(
        src_ref=emb_hbm.at[:, :, pl.ds(pl.multiple_of((1 - core) * half, 128), half)], dst_ref=theirs,
        send_sem=swap_sem.at[0], recv_sem=swap_sem.at[1], device_id=sibling, device_id_type=MESH,
    )
    swap.start()

    packed_corner = sum(cornered[c] << (4 * c) for c in chips)
    chip = [partner_of(me, 2 * e, members) // 2 for e in range(4)]
    bits = [[named_of(2 * chip[e] + t) for t in (0, 1)] for e in range(4)]

    def corner_of(c):
        return (packed_corner >> (4 * c)) & 15

    def turn_of(c):
        return (best >> (2 * c)) & 3

    def hop(e, link):
        if link == 0:
            return turn_of(chip[e]), corner_of(chip[e ^ 2]) - turn_of(chip[e ^ 2])
        return corner_of(chip[e]) - turn_of(chip[e]), turn_of(chip[e ^ 1])

    def flag(src, s, dst, t):
        return (bits[dst][t] >> (2 * chip[src] + s)) & 1

    def pick(src, dst):
        total = jnp.int32(0)
        for k in range(in_slots):
            total += same(owners[k, dst], src) * blocks[k, dst]
        return total

    def placed(at, relays):
        return jnp.minimum(at + jnp.where(at >= 2, relays, 0), 7)

    codes = [jnp.int32(0), jnp.int32(0)]

    def code_of(s, e, t):
        apart = core + s - 2 * core * s
        return pick(2 * chip[0] + s, 2 * chip[e] + t) + block_count * apart

    for link, e in LINKS_OUT:
        at, relays = hop(0, link)
        table[AT_RELAYS + link] = relays
        for t in (0, 1):
            for s in (0, 1):
                there = flag(0, s, e, t)
                codes[link] += there * jnp.left_shift(code_of(s, e, t), 4 * placed(at, relays))
                at += there
    at = jnp.int32(0)
    for t in (0, 1):
        for s in (0, 1):
            there = flag(0, s, 3, t)
            code = code_of(s, 3, t)
            split = turn_of(chip[0])
            early = jnp.where(at < split, there, 0)
            codes[0] += early * jnp.left_shift(code, 4 * jnp.minimum(at, 7))
            codes[1] += (there - early) * jnp.left_shift(code, 4 * jnp.maximum(at - split, 0))
            at += there
    for link in (0, 1):
        table[AT_CODES + link] = codes[link]

    wanted = [owners[k, me] for k in range(in_slots)]
    places = [same(q, partner_of(me, 1, members)) * 16 for q in wanted]
    for e in (1, 2, 3):
        flags = [[flag(e, s, 0, t) for s in (0, 1)] for t in (0, 1)]
        for s in (0, 1):
            ahead = core * (flags[0][0] + flags[0][1])
            if s == 1:
                ahead += jnp.where(core == 0, flags[0][0], flags[1][0])
            if e < 3:
                link = e - 1
                begin, relays = hop(e, link)
                place = 8 * link + placed(begin + ahead, relays)
            else:
                split = turn_of(chip[3])
                place = jnp.where(ahead < split, 8 + RELAY[0] + ahead, RELAY[0] + ahead - split)
            for k in range(in_slots):
                places[k] += same(wanted[k], 2 * chip[e] + s) * place
    for k in range(in_slots):
        table[AT_PLACE + k] = places[k]
        index = jnp.int32(0)
        for mask in range(1, members):
            index += same(wanted[k], partner_of(me, mask, members)) * (mask + 1)
        table[AT_SUM + k] = index
    for mask in range(1, members):
        table[AT_PICK + mask - 1] = pick(me, partner_of(me, mask, members))
    for i in range(AT_PICK + members - 1, TABLE):
        table[i] = jnp.int32(0)

    most = mine[...]
    for i, copy in enumerate(copies):
        copy.wait()
        most = jnp.maximum(most, others[i])
    table[0] = jnp.max(most)
    swap.wait()


def route(owners, blocks, emb, group_count):
    smem = pl.BlockSpec(memory_space=pltpu.SMEM)
    any_space = pl.BlockSpec(memory_space=pl.ANY)
    block_count, block_rows, features = emb.shape
    others = max(group_count - 1, 1)
    return pl.pallas_call(
        functools.partial(route_kernel, group_count, block_count),
        out_shape=(
            jax.ShapeDtypeStruct((TABLE,), jnp.int32),
            jax.ShapeDtypeStruct((block_count, block_rows, features // 2), emb.dtype),
        ),
        in_specs=[smem] * 2 + [any_space],
        out_specs=(smem, any_space),
        scratch_shapes=[
            pltpu.VMEM((8, 128), jnp.int32),
            pltpu.VMEM((others, 8, 128), jnp.int32),
            pltpu.SemaphoreType.DMA((others,)),
            pltpu.SemaphoreType.DMA((others,)),
            pltpu.SemaphoreType.DMA((2,)),
        ],
        compiler_params=pltpu.CompilerParams(collective_id=0, has_side_effects=True),
    )(owners, blocks, emb)


def halves_of(classes):
    half = -(-classes // 16) * 8
    low = -(-half // 32) * 16
    return half, (low, half - low)


def spread_kernel(
    cap, member_count, group_count,
    table, cross, emb_hbm, theirs_hbm, prior_hbm, links_hbm, out, row_sums,
    share, links, scores, weights, mix, sums, sum_send, sum_recv,
    own_low, own_high, keys_low, keys_high, key_emb, *rest,
):
    unit_refs, (load_sem, ex_sem, slot_sem, fwd_sem, near_sem, far_sem, sum_sem) = rest[:-7], rest[-7:]
    group = lax.axis_index("group")
    me = lax.axis_index("member")
    core = me % 2
    sibling = (group, partner_of(me, 1, member_count))
    nexts = [(group, partner_of(me, 2, member_count)), (group, partner_of(me, 4, member_count))]
    ends = [((group + 1) % group_count, me), ((group + group_count - 1) % group_count, me)]
    partners = [(group, partner_of(me, mask, member_count)) for mask in range(1, member_count)]
    everyone = ends + partners
    _, half, rows = share.shape
    classes = out.shape[0]
    block_count = rows // BR
    heights = (own_low.shape[1], own_high.shape[1])
    bands = (slice(0, heights[0]), slice(heights[0], half))
    twice = 2 * half - classes
    owns, keys = (own_low, own_high), (keys_low, keys_high)
    width = 2 * BR if block_count % 2 == 0 else BR
    in_chunk = width // BR
    chunks = rows // width
    near_at = rows + 2 * BR
    near = 4
    offsets = [(classes - half) * core, (classes - half) * (1 - core)]
    order = FIRST + tuple(range(PURE, cap))
    slots = tuple((link, s) for s in range(cap) for link in (0, 1))

    started = {}

    class Copy:
        def __init__(self, src, dst, sems, at, device):
            self.key = (id(sems), at)
            self.copy = pltpu.make_async_remote_copy(
                src_ref=src, dst_ref=dst, send_sem=sems.at[(0,) + at], recv_sem=sems.at[(1,) + at],
                device_id=device, device_id_type=MESH,
            )

        def start(self):
            started[self.key] = self
            self.copy.start()

        def wait_recv(self):
            self.copy.wait_recv()

        def wait_send(self):
            self.copy.wait_send()

    class Unit:
        def __init__(self, index, refs):
            self.index = index
            self.mine, self.oth, self.theirs, self.send, self.recv, self.fwd, self.near, self.far, self.far_in = refs

        def ex(self):
            return Copy(self.oth, self.theirs, ex_sem, (self.index,), sibling)

        def slot(self, link, s):
            i = link * cap + s
            return Copy(self.send.at[i], self.recv.at[i], slot_sem, (self.index, i), nexts[link])

        def forward(self, link, s):
            i = link * cap + s
            return Copy(self.recv.at[i], self.fwd.at[i], fwd_sem, (self.index, i), sibling)

        def sib(self, part):
            dst = self.recv if part == 1 else self.fwd
            return Copy(self.near.at[part], dst.at[2 * cap], near_sem, (self.index, part), sibling)

        def cross(self, i):
            return Copy(self.far.at[i], self.far_in.at[i], far_sem, (self.index, i), ends[i])

        def block_of(self, code):
            own = self.mine[jnp.minimum(code, block_count - 1)]
            return jnp.where(code < block_count, own, self.theirs[jnp.maximum(code - block_count, 0)])

    units = [Unit(i, unit_refs[9 * i:9 * i + 9]) for i in range(1 + 2 * ITERS)]
    emb = units[0]
    labels = [units[1 + 2 * stage:3 + 2 * stage] for stage in range(ITERS)]

    loads = [
        pltpu.make_async_copy(
            emb_hbm.at[:, :, pl.ds(pl.multiple_of(core * emb.oth.shape[2], 128), emb.oth.shape[2])],
            emb.mine, load_sem.at[0],
        ),
        pltpu.make_async_copy(
            emb_hbm.at[:, :, pl.ds(pl.multiple_of((1 - core) * emb.oth.shape[2], 128), emb.oth.shape[2])],
            emb.oth, load_sem.at[1],
        ),
        pltpu.make_async_copy(
            prior_hbm.at[pl.ds(pl.multiple_of(offsets[0], 8), half)], share.at[0], load_sem.at[2]
        ),
        pltpu.make_async_copy(
            prior_hbm.at[pl.ds(pl.multiple_of(offsets[1], 8), half)], share.at[1], load_sem.at[3]
        ),
        pltpu.make_async_copy(links_hbm, links, load_sem.at[4]),
        pltpu.make_async_copy(theirs_hbm, emb.theirs, load_sem.at[5]),
    ]
    for i in (0, 5, 1, 2, 3, 4):
        loads[i].start()
    barrier = pltpu.get_barrier_semaphore()
    for target in everyone:
        pl.semaphore_signal(barrier, inc=1, device_id=target, device_id_type=MESH)

    codes = [[(table[AT_CODES + link] >> (4 * s)) & 15 for s in range(cap)] for link in (0, 1)]
    relays = [table[AT_RELAYS + link] for link in (0, 1)]
    places = []
    for k in range(near):
        place = table[AT_PLACE + k]
        places.append(jnp.minimum(place % 8 + cap * (place // 8), 2 * cap))
    picks = [cross[0, ends[0][0]], cross[1, ends[1][0]]]
    picks += [table[AT_PICK + i] for i in range(member_count - 1)]
    sum_at = [table[AT_SUM + k] for k in range(near)]

    def side(unit):
        for part, ref in ((0, unit.mine), (1, unit.oth)):
            unit.near[part] = ref[picks[2]]
            unit.sib(part).start()
        for i in (0, 1):
            unit.far[i, 0] = unit.mine[picks[i]]
            unit.far[i, 1] = unit.oth[picks[i]]
            unit.cross(i).start()

    def first(unit):
        if unit is not emb:
            unit.ex().wait_recv()
        for s in order:
            for link in (0, 1):
                unit.send[link * cap + s] = unit.block_of(codes[link][s])
                unit.slot(link, s).start()

    def relay(unit):
        for s in FIRST:
            for link in (0, 1):
                unit.slot(link, s).wait_recv()
        for s in FIRST:
            for link in (0, 1):
                passing = unit.recv[(1 - link) * cap + s]
                unit.send[link * cap + RELAY[s]] = jnp.where(
                    s < relays[link], passing, unit.block_of(codes[link][RELAY[s]])
                )
                unit.slot(link, RELAY[s]).start()
        for s in FIRST:
            for link in (0, 1):
                unit.forward(link, s).start()

    def pass_on(unit, which):
        for s in which:
            for link in (0, 1):
                unit.slot(link, s).wait_recv()
                unit.forward(link, s).start()

    pure = tuple(range(PURE, cap))

    def gathered(unit):
        for link, s in slots:
            unit.forward(link, s).wait_recv()
        for part in (0, 1):
            unit.sib(part).wait_recv()

    loads[0].wait()
    loads[5].wait()
    pl.semaphore_wait(barrier, len(everyone))
    first(emb)
    loads[1].wait()
    side(emb)
    loads[2].wait()
    loads[3].wait()

    def lanes_of(c):
        return pl.ds(pl.multiple_of(c * width, width), width)

    def summed(value, part, t):
        if part == 0 or twice == 0:
            return jnp.sum(value, axis=0, keepdims=True)
        if t == 0:
            rest, again, count = value[twice:], value[:twice], core
        else:
            rest, again, count = value[:-twice], value[-twice:], 1 - core
        total = jnp.sum(rest, axis=0, keepdims=True)
        return total + jnp.sum(again, axis=0, keepdims=True) * count.astype(jnp.float32)

    def put_blocks(stage, part, t, c, value):
        unit = labels[stage][t]
        ref = unit.oth if part else unit.mine
        for b in range(in_chunk):
            ref[c * in_chunk + b] = value[:, b * BR:(b + 1) * BR]

    def first_labels(c, _):
        lanes = lanes_of(c)
        total = jnp.zeros((1, width), jnp.float32)
        for part in (0, 1):
            for t in (0, 1):
                total += summed(share[part, bands[t], lanes], part, t)
        scale = 1.0 / total
        for part in (0, 1):
            for t in (0, 1):
                value = share[part, bands[t], lanes] * scale
                share[part, bands[t], lanes] = value
                value = value.astype(jnp.bfloat16)
                owns[t][part, :, lanes] = value
                put_blocks(0, part, t, c, value)
        return _

    lax.fori_loop(0, chunks, first_labels, 0)
    for t in (0, 1):
        labels[0][t].ex().start()
        side(labels[0][t])

    features = 2 * emb.oth.shape[2]

    def score_rows(at, low, high, finish):
        height = low.shape[0]

        def body(c, _):
            lanes = lanes_of(c)
            picked = pl.ds(c * in_chunk, in_chunk)
            value = sum(
                lax.dot_general(
                    keys, ref[picked].reshape(width, features // 2), (((1,), (1,)), ((), ())),
                    preferred_element_type=jnp.float32,
                )
                for keys, ref in ((low[...], emb.mine), (high[...], emb.oth))
            )
            scores[at:at + height, lanes] = finish(value * features ** (-0.5), c, lanes)
            return _

        lax.fori_loop(0, chunks, body, 0)

    def off_diagonal(value, c, lanes):
        key_ids = lax.broadcasted_iota(jnp.int32, (rows, width), 0)
        row_ids = lax.broadcasted_iota(jnp.int32, (rows, width), 1) + c * width
        return jnp.where(key_ids != row_ids, value, -jnp.inf)

    def linked(names):
        def finish(value, c, lanes):
            parts = []
            for i, name in enumerate(names):
                bias = jnp.max(jnp.where(links[:, lanes] == name, 0.0, -jnp.inf), axis=0, keepdims=True)
                parts.append(value[i * BR:(i + 1) * BR] + bias)
            return jnp.concatenate(parts, axis=0)

        return finish

    for b in range(block_count):
        key_emb[0, b * BR:(b + 1) * BR] = emb.mine[b]
        key_emb[1, b * BR:(b + 1) * BR] = emb.oth[b]
    score_rows(0, key_emb.at[0], key_emb.at[1], off_diagonal)
    loads[4].wait()

    relay(emb)
    pass_on(emb, pure)
    first(labels[0][0])
    for i in (0, 1):
        emb.cross(i).wait_recv()
        for part in (0, 1):
            key_emb[part, i * BR:(i + 1) * BR] = emb.far_in[i, part]
    low, high = (key_emb.at[part, pl.ds(0, 2 * BR)] for part in (0, 1))
    score_rows(rows, low, high, linked((near, near + 1)))
    pass_on(emb, RELAY)
    gathered(emb)
    for k in range(near):
        for part, ref in ((0, emb.recv), (1, emb.fwd)):
            key_emb[part, k * BR:(k + 1) * BR] = ref[places[k]]
    relay(labels[0][0])
    first(labels[0][1])
    low, high = (key_emb.at[part, pl.ds(0, near * BR)] for part in (0, 1))
    score_rows(near_at, low, high, linked(range(near)))

    def soften(b, _):
        lanes = pl.ds(pl.multiple_of(b * BR, BR), BR)
        value = scores[:, lanes]
        powers = jnp.exp(value - jnp.max(value, axis=0, keepdims=True))
        total = jnp.sum(powers, axis=0, keepdims=True)
        weights[:, lanes] = (powers * (1.0 / total)).astype(jnp.bfloat16)
        return _

    lax.fori_loop(0, block_count, soften, 0)

    def scaled(block, at):
        return (block.astype(jnp.float32) * (1.0 / sum_recv[at][:1])).astype(jnp.bfloat16)

    def premix(stage, t):
        unit = labels[stage][t]
        for i in (0, 1):
            unit.cross(i).wait_recv()
            for part in (0, 1):
                block = unit.far_in[i, part]
                owns[t][part, :, rows + i * BR:rows + (i + 1) * BR] = scaled(block, i) if stage else block

        def body(c, _):
            lanes = lanes_of(c)
            for part in (0, 1):
                mix[part, bands[t], lanes] = jnp.dot(
                    owns[t][part], weights[:near_at, lanes], preferred_element_type=jnp.float32
                )
            return _

        lax.fori_loop(0, chunks, body, 0)

    def neighbour_mix(stage, t, finish):
        unit = labels[stage][t]
        gathered(unit)
        for k in range(near):
            for part, ref in ((0, unit.recv), (1, unit.fwd)):
                block = ref[places[k]]
                keys[t][part, :, k * BR:(k + 1) * BR] = scaled(block, sum_at[k]) if stage else block

        def body(c, _):
            lanes = lanes_of(c)
            total_sum = jnp.zeros((1, width), jnp.float32)
            for part in (0, 1):
                total = mix[part, bands[t], lanes] + jnp.dot(
                    keys[t][part], weights[near_at:, lanes], preferred_element_type=jnp.float32
                )
                mixed = MIXING * total + (1.0 - MIXING) * share[part, bands[t], lanes]
                squared = mixed * mixed
                total_sum += summed(squared, part, t)
                finish(c, lanes, part, squared)
            for b in range(in_chunk):
                value = jnp.broadcast_to(total_sum[:, b * BR:(b + 1) * BR], (8, BR))
                at = c * in_chunk + b
                sums[at] = value if t == 0 else sums[at] + value
            return _

        lax.fori_loop(0, chunks, body, 0)

    def middle(stage, t):
        def finish(c, lanes, part, squared):
            mix[part, bands[t], lanes] = squared
            put_blocks(stage + 1, part, t, c, squared.astype(jnp.bfloat16))

        return finish

    def last(t):
        def finish(c, lanes, part, squared):
            begin = pl.multiple_of(offsets[part] + bands[t].start, 8)
            out[pl.ds(begin, heights[t]), lanes] = squared

        return finish

    def sum_copy(s):
        return Copy(sum_send.at[s], sum_recv.at[s], sum_sem, (s,), everyone[s])

    def own_labels(c, _):
        lanes = lanes_of(c)
        parts = [sums[c * in_chunk + b][:1] for b in range(in_chunk)]
        scale = 1.0 / jnp.concatenate(parts, axis=1)
        for part in (0, 1):
            for t in (0, 1):
                owns[t][part, :, lanes] = (mix[part, bands[t], lanes] * scale).astype(jnp.bfloat16)
        return _

    for stage in range(ITERS):
        final = stage == ITERS - 1
        this = labels[stage]
        premix(stage, 0)
        if final:
            premix(stage, 1)
        pass_on(this[0], pure + RELAY)
        if not final:
            relay(this[1])
        neighbour_mix(stage, 0, last(0) if final else middle(stage, 0))
        if final:
            relay(this[1])
        else:
            later = labels[stage + 1]
            later[0].ex().start()
            side(later[0])
            premix(stage, 1)
            first(later[0])
        pass_on(this[1], pure + RELAY)
        neighbour_mix(stage, 1, last(1) if final else middle(stage, 1))
        if not final:
            for s in range(len(everyone)):
                sum_send[s] = sums[picks[s]]
                sum_copy(s).start()
            later[1].ex().start()
            side(later[1])
            relay(later[0])
            first(later[1])
            lax.fori_loop(0, chunks, own_labels, 0)
            for s in range(len(everyone)):
                sum_copy(s).wait_recv()

    for b in range(block_count):
        row_sums[:, b * BR:(b + 1) * BR] = sums[b]
    for copy in started.values():
        copy.wait_send()


def spread(cap, member_count, group_count, table, cross, emb, theirs, prior, links):
    block_count, _, features = emb.shape
    classes, rows = prior.shape
    half, heights = halves_of(classes)
    any_space = pl.BlockSpec(memory_space=pl.ANY)
    smem = pl.BlockSpec(memory_space=pltpu.SMEM)
    vmem = pl.BlockSpec(memory_space=pltpu.VMEM)
    bf16, f32 = jnp.bfloat16, jnp.float32
    keys = rows + 6 * BR
    partners = member_count + 1

    def unit(height, wide):
        counts = (
            (block_count,), (block_count,), (block_count,), (2 * cap,), (2 * cap + 1,), (2 * cap + 1,), (2,), (2, 2), (2, 2)
        )
        return [pltpu.VMEM(count + (height, wide), bf16) for count in counts]

    def dma(*shape):
        return pltpu.SemaphoreType.DMA((2,) + shape)

    units = 1 + 2 * ITERS
    return pl.pallas_call(
        functools.partial(spread_kernel, cap, member_count, group_count),
        out_shape=(pltpu.VMEM((classes, rows), f32), pltpu.VMEM((8, rows), f32)),
        in_specs=[smem] * 2 + [any_space] * 4,
        out_specs=(vmem, vmem),
        scratch_shapes=[
            pltpu.VMEM((2, half, rows), f32),
            pltpu.VMEM((links.shape[0], rows), jnp.int32),
            pltpu.VMEM((keys, rows), f32),
            pltpu.VMEM((keys, rows), bf16),
            pltpu.VMEM((2, half, rows), f32),
            pltpu.VMEM((block_count, 8, BR), f32),
            pltpu.VMEM((partners, 8, BR), f32),
            pltpu.VMEM((partners, 8, BR), f32),
            pltpu.VMEM((2, heights[0], rows + 2 * BR), bf16),
            pltpu.VMEM((2, heights[1], rows + 2 * BR), bf16),
            pltpu.VMEM((2, heights[0], 4 * BR), bf16),
            pltpu.VMEM((2, heights[1], 4 * BR), bf16),
            pltpu.VMEM((2, rows, features // 2), bf16),
            *unit(BR, features // 2),
            *(ref for _ in range(ITERS) for height in heights for ref in unit(height, BR)),
            pltpu.SemaphoreType.DMA((6,)),
            dma(units), dma(units, 2 * cap), dma(units, 2 * cap), dma(units, 2), dma(units, 2), dma(partners),
        ],
        compiler_params=pltpu.CompilerParams(
            collective_id=cap, has_side_effects=True, vmem_limit_bytes=60 * 2**20
        ),
    )(table, cross, emb, theirs, prior, links)


def spread_body(embeddings, prior, source_member, source_block, cross_block, row_links):
    member_count = lax.axis_size("member")
    group_count = lax.axis_size("group")
    rows, features = embeddings.shape
    emb_blocks = embeddings.reshape(rows // BR, BR, features)
    table, theirs = route(source_member[0].T, source_block[0].T, emb_blocks, group_count)
    caps = (6, 7, 8)
    branches = [functools.partial(spread, cap, member_count, group_count) for cap in caps]
    squared, sums = lax.switch(
        jnp.clip(table[0] - caps[0], 0, len(caps) - 1), branches,
        table, cross_block[:, 0, :].T, emb_blocks, theirs, prior.T, row_links.T,
    )
    return (squared * (prior.shape[1] / sums[:1])).T


def solution(mesh):
    spread_fits = mesh.shape["member"] == 8
    body = spread_body if spread_fits else relay_body
    placed = (
        P(("group", "member"), None),
        P(("group", "member"), None),
        P("group", None, None),
        P("group", None, None),
        P(None, "member", None),
        P(("group", "member"), None),
    )
    return jax.shard_map(
        body, mesh=mesh, in_specs=placed, out_specs=P(("group", "member"), None), check_vma=False
    )
```

```python
import functools

import jax
import jax.numpy as jnp
from jax import lax
from jax.experimental import pallas as pl
from jax.experimental.pallas import tpu as pltpu
from jax.sharding import PartitionSpec as P

BR = 128
SERVE_CAP = 7
ITERS = 2


MIXING = 0.8


def extended(value, sides, width):
    for axis, dim in sides:
        size, length = (lax.axis_size(axis), value.shape[dim])
        up = [(i, (i + 1) % size) for i in range(size)]
        down = [(j, i) for i, j in up]
        last = lax.slice_in_dim(value, length - width, length, axis=dim)
        first = lax.slice_in_dim(value, 0, width, axis=dim)
        before = lax.ppermute(last, axis, up)
        after = lax.ppermute(first, axis, down)
        value = jnp.concatenate([before, value, after], axis=dim)
    return value


def allowed_mask(row_links, near_total, slot_total, row_count, block_rows):
    slot_ids = jnp.arange(slot_total, dtype=jnp.int32)
    slot_hits = jnp.any(row_links[:, :, None] == slot_ids[None, None, :], axis=1)
    near_mask = jnp.tile(slot_hits[:, :near_total], (1, block_rows))
    far_mask = jnp.repeat(slot_hits[:, near_total:], block_rows, axis=1)
    row_ids = lax.broadcasted_iota(jnp.int32, (row_count, row_count), 0)
    col_ids = lax.broadcasted_iota(jnp.int32, (row_count, row_count), 1)
    local_mask = row_ids != col_ids
    return jnp.concatenate([local_mask, near_mask, far_mask], axis=1)


def kernel_weights(queries, key_rows, allowed):
    features = queries.shape[1]
    scores = lax.dot_general(
        queries, key_rows, (((1,), (1,)), ((), ())), preferred_element_type=jnp.float32
    )
    scores = scores * features ** (-0.5)
    scores = jnp.where(allowed, scores, -jnp.inf)
    highest = jnp.max(scores, axis=1, keepdims=True)
    powers = jnp.where(allowed, jnp.exp(scores - highest), 0.0)
    return (powers / jnp.sum(powers, axis=1, keepdims=True)).astype(jnp.bfloat16)


def sharpen(weights, key_labels, prior_share):
    mixed = (
        MIXING * jnp.dot(weights, key_labels, preferred_element_type=jnp.float32)
        + (1.0 - MIXING) * prior_share
    )
    squared = mixed * mixed
    return squared / jnp.sum(squared, axis=1, keepdims=True)


def one_hot(ids, count):
    return (ids[..., None] == jnp.arange(count, dtype=jnp.int32)).astype(jnp.bfloat16)


def near_keys(delivered):
    return delivered.reshape(-1, delivered.shape[-1])


def far_keys(padded):
    return jnp.concatenate([padded[0], padded[-1]], axis=0)


def relay_body(embeddings, prior, source_member, source_block, cross_block, row_links):
    member_count = lax.axis_size("member")
    group_count = lax.axis_size("group")
    group_index = lax.axis_index("group")
    member_index = lax.axis_index("member")
    row_count, features = embeddings.shape
    classes = prior.shape[1]
    block_rows = BR
    block_count = row_count // block_rows
    piece_rows = block_rows // member_count
    owners = source_member[0]
    slot_count = owners.shape[1]
    flat_owner = owners.reshape(-1)
    flat_block = source_block[0].reshape(-1)
    order_ids = jnp.arange(flat_owner.shape[0], dtype=jnp.int32)
    earlier = (flat_owner[:, None] == flat_owner[None, :]) & (
        order_ids[None, :] < order_ids[:, None]
    )
    rank_ids = jnp.sum(earlier.astype(jnp.int32), axis=1)
    serve_ids = jnp.arange(SERVE_CAP, dtype=jnp.int32)
    serving = (flat_owner[None, :] == member_index) & (rank_ids[None, :] == serve_ids[:, None])
    served_blocks = jnp.sum(jnp.where(serving, flat_block[None, :], 0), axis=1)
    served_hot = one_hot(served_blocks, block_count)
    rank_grid = rank_ids.reshape(member_count, slot_count)
    deliver_hot = one_hot(owners, member_count)[..., :, None] * one_hot(rank_grid, SERVE_CAP)[..., None, :]
    below_group = (group_index + group_count - 1) % group_count
    above_group = (group_index + 1) % group_count
    group_ids = jnp.arange(group_count, dtype=jnp.int32)
    cross_pick = jnp.stack([
        jnp.sum(jnp.where(group_ids == below_group, cross_block[:, 0, 1], 0)),
        jnp.sum(jnp.where(group_ids == above_group, cross_block[:, 0, 0], 0)),
    ])
    cross_hot = one_hot(cross_pick, block_count)
    allowed = allowed_mask(
        row_links, slot_count, slot_count + cross_block.shape[2], row_count, block_rows
    )
    prior_share = prior / jnp.sum(prior, axis=1, keepdims=True)
    labels = prior_share.astype(jnp.bfloat16)
    emb_blocks = embeddings.reshape(block_count, block_rows, features)

    def cross_of(blocks):
        return jnp.einsum("cb,brl->crl", cross_hot, blocks, preferred_element_type=jnp.float32).astype(jnp.bfloat16)

    def relay_pieces(flat_rows):
        blocks = flat_rows.reshape(block_count, member_count, piece_rows, flat_rows.shape[-1])
        return jnp.einsum("sb,bmpl->mpsl", served_hot, blocks, preferred_element_type=jnp.float32).astype(jnp.bfloat16)

    def deliver_pieces(received):
        return jnp.einsum("mkos,opsl->mpkl", deliver_hot, received, preferred_element_type=jnp.float32).astype(jnp.bfloat16)

    result = prior_share
    emb_relay = lax.all_to_all(
        relay_pieces(embeddings), "member", split_axis=0, concat_axis=0, tiled=True
    )
    emb_near = lax.all_to_all(
        deliver_pieces(emb_relay), "member", split_axis=0, concat_axis=0, tiled=True
    )
    emb_far = extended(cross_of(emb_blocks), (("group", 0),), 1)
    key_rows = jnp.concatenate([embeddings, near_keys(emb_near), far_keys(emb_far)], axis=0)
    weights = kernel_weights(embeddings, key_rows, allowed)
    for iteration in range(ITERS):
        lab_blocks = labels.reshape(block_count, block_rows, classes)
        lab_relay = lax.all_to_all(
            relay_pieces(labels), "member", split_axis=0, concat_axis=0, tiled=True
        )
        lab_near = lax.all_to_all(
            deliver_pieces(lab_relay), "member", split_axis=0, concat_axis=0, tiled=True
        )
        lab_far = extended(cross_of(lab_blocks), (("group", 0),), 1)
        key_labels = jnp.concatenate([labels, near_keys(lab_near), far_keys(lab_far)], axis=0)
        result = sharpen(weights, key_labels, prior_share)
        labels = result.astype(jnp.bfloat16)
    return result * classes


MESH = pl.DeviceIdType.MESH
TABLE = 32
AT_CODES, AT_RELAYS, AT_PLACE, AT_SUM, AT_PICK = 1, 3, 5, 9, 13
FIRST, RELAY, PURE = (0, 1), (2, 3), 4
LINKS_OUT = ((0, 1), (1, 2))


def partner_of(member, mask, member_count):
    bit = 1
    while bit < member_count:
        if mask & bit:
            member = member + bit - 2 * bit * (member // bit % 2)
        bit *= 2
    return member


def same(left, right):
    gap = left - right
    return 1 - jnp.minimum(gap * gap, 1)


def pairs_in(bits):
    return bits - (bits >> 1)


def route_kernel(
    group_count, block_count, owners, blocks, emb_hbm, table, theirs, mine, others, send_sem, recv_sem, swap_sem
):
    group = lax.axis_index("group")
    me = lax.axis_index("member")
    core = me % 2
    in_slots, members = owners.shape
    targets = [((group + i) % group_count, me) for i in range(1, group_count)]
    sibling = (group, partner_of(me, 1, members))
    barrier = pltpu.get_barrier_semaphore()
    for target in targets + [sibling]:
        pl.semaphore_signal(barrier, inc=1, device_id=target, device_id_type=MESH)

    def named_of(p):
        bits = jnp.int32(0)
        for k in range(in_slots):
            bits += jnp.left_shift(jnp.int32(1), owners[k, p])
        return bits

    named = [named_of(p) for p in range(members)]

    def flow(src, dst):
        return sum(pairs_in((named[2 * dst + t] >> (2 * src)) & 3) for t in (0, 1))

    chips = range(members // 2)
    flat = [[flow(c, c ^ 1), flow(c, c ^ 2)] for c in chips]
    cornered = [flow(c, c ^ 3) for c in chips]
    choice = lax.broadcasted_iota(jnp.int32, (8, 128), 0) * 128 + lax.broadcasted_iota(jnp.int32, (8, 128), 1)
    choice = choice & 255
    turn = [(choice >> (2 * c)) & 3 for c in chips]
    fits = choice >= 0
    load = jnp.zeros_like(choice)
    for c in chips:
        fits &= (turn[c] <= 2) & (turn[c] <= cornered[c]) & (turn[c] >= cornered[c] - 2)
        load = jnp.maximum(load, turn[c] - turn[c ^ 2] + (flat[c][0] + cornered[c ^ 2]))
        load = jnp.maximum(load, turn[c ^ 1] - turn[c] + (flat[c][1] + cornered[c]))
    best = jnp.min(jnp.where(fits, load * 256 + choice, 1 << 20))
    need = best >> 8

    mine[...] = jnp.full(mine.shape, need, jnp.int32)
    pl.semaphore_wait(barrier, len(targets) + 1)
    copies = []
    for i, target in enumerate(targets):
        copy = pltpu.make_async_remote_copy(
            src_ref=mine, dst_ref=others.at[i], send_sem=send_sem.at[i], recv_sem=recv_sem.at[i],
            device_id=target, device_id_type=MESH,
        )
        copy.start()
        copies.append(copy)

    half = theirs.shape[2]
    swap = pltpu.make_async_remote_copy(
        src_ref=emb_hbm.at[:, :, pl.ds(pl.multiple_of((1 - core) * half, 128), half)], dst_ref=theirs,
        send_sem=swap_sem.at[0], recv_sem=swap_sem.at[1], device_id=sibling, device_id_type=MESH,
    )
    swap.start()

    packed_corner = sum(cornered[c] << (4 * c) for c in chips)
    chip = [partner_of(me, 2 * e, members) // 2 for e in range(4)]
    bits = [[named_of(2 * chip[e] + t) for t in (0, 1)] for e in range(4)]

    def corner_of(c):
        return (packed_corner >> (4 * c)) & 15

    def turn_of(c):
        return (best >> (2 * c)) & 3

    def hop(e, link):
        if link == 0:
            return turn_of(chip[e]), corner_of(chip[e ^ 2]) - turn_of(chip[e ^ 2])
        return corner_of(chip[e]) - turn_of(chip[e]), turn_of(chip[e ^ 1])

    def flag(src, s, dst, t):
        return (bits[dst][t] >> (2 * chip[src] + s)) & 1

    def pick(src, dst):
        total = jnp.int32(0)
        for k in range(in_slots):
            total += same(owners[k, dst], src) * blocks[k, dst]
        return total

    def placed(at, relays):
        return jnp.minimum(at + jnp.where(at >= 2, relays, 0), 7)

    codes = [jnp.int32(0), jnp.int32(0)]

    def code_of(s, e, t):
        apart = core + s - 2 * core * s
        return pick(2 * chip[0] + s, 2 * chip[e] + t) + block_count * apart

    for link, e in LINKS_OUT:
        at, relays = hop(0, link)
        table[AT_RELAYS + link] = relays
        for t in (0, 1):
            for s in (0, 1):
                there = flag(0, s, e, t)
                codes[link] += there * jnp.left_shift(code_of(s, e, t), 4 * placed(at, relays))
                at += there
    at = jnp.int32(0)
    for t in (0, 1):
        for s in (0, 1):
            there = flag(0, s, 3, t)
            code = code_of(s, 3, t)
            split = turn_of(chip[0])
            early = jnp.where(at < split, there, 0)
            codes[0] += early * jnp.left_shift(code, 4 * jnp.minimum(at, 7))
            codes[1] += (there - early) * jnp.left_shift(code, 4 * jnp.maximum(at - split, 0))
            at += there
    for link in (0, 1):
        table[AT_CODES + link] = codes[link]

    wanted = [owners[k, me] for k in range(in_slots)]
    places = [same(q, partner_of(me, 1, members)) * 16 for q in wanted]
    for e in (1, 2, 3):
        flags = [[flag(e, s, 0, t) for s in (0, 1)] for t in (0, 1)]
        for s in (0, 1):
            ahead = core * (flags[0][0] + flags[0][1])
            if s == 1:
                ahead += jnp.where(core == 0, flags[0][0], flags[1][0])
            if e < 3:
                link = e - 1
                begin, relays = hop(e, link)
                place = 8 * link + placed(begin + ahead, relays)
            else:
                split = turn_of(chip[3])
                place = jnp.where(ahead < split, 8 + RELAY[0] + ahead, RELAY[0] + ahead - split)
            for k in range(in_slots):
                places[k] += same(wanted[k], 2 * chip[e] + s) * place
    for k in range(in_slots):
        table[AT_PLACE + k] = places[k]
        index = jnp.int32(0)
        for mask in range(1, members):
            index += same(wanted[k], partner_of(me, mask, members)) * (mask + 1)
        table[AT_SUM + k] = index
    for mask in range(1, members):
        table[AT_PICK + mask - 1] = pick(me, partner_of(me, mask, members))
    for i in range(AT_PICK + members - 1, TABLE):
        table[i] = jnp.int32(0)

    most = mine[...]
    for i, copy in enumerate(copies):
        copy.wait()
        most = jnp.maximum(most, others[i])
    table[0] = jnp.max(most)
    swap.wait()


def route(owners, blocks, emb, group_count):
    smem = pl.BlockSpec(memory_space=pltpu.SMEM)
    any_space = pl.BlockSpec(memory_space=pl.ANY)
    block_count, block_rows, features = emb.shape
    others = max(group_count - 1, 1)
    return pl.pallas_call(
        functools.partial(route_kernel, group_count, block_count),
        out_shape=(
            jax.ShapeDtypeStruct((TABLE,), jnp.int32),
            jax.ShapeDtypeStruct((block_count, block_rows, features // 2), emb.dtype),
        ),
        in_specs=[smem] * 2 + [any_space],
        out_specs=(smem, any_space),
        scratch_shapes=[
            pltpu.VMEM((8, 128), jnp.int32),
            pltpu.VMEM((others, 8, 128), jnp.int32),
            pltpu.SemaphoreType.DMA((others,)),
            pltpu.SemaphoreType.DMA((others,)),
            pltpu.SemaphoreType.DMA((2,)),
        ],
        compiler_params=pltpu.CompilerParams(collective_id=0, has_side_effects=True),
    )(owners, blocks, emb)


def halves_of(classes):
    half = -(-classes // 16) * 8
    low = -(-half // 32) * 16
    return half, (low, half - low)


def spread_kernel(
    cap, member_count, group_count,
    table, cross, emb_hbm, theirs_hbm, prior_hbm, links_hbm, out, row_sums,
    share, links, scores, weights, mix, sums, sum_send, sum_recv,
    own_low, own_high, keys_low, keys_high, key_emb, *rest,
):
    unit_refs, (load_sem, ex_sem, slot_sem, fwd_sem, near_sem, far_sem, sum_sem) = rest[:-7], rest[-7:]
    group = lax.axis_index("group")
    me = lax.axis_index("member")
    core = me % 2
    sibling = (group, partner_of(me, 1, member_count))
    nexts = [(group, partner_of(me, 2, member_count)), (group, partner_of(me, 4, member_count))]
    ends = [((group + 1) % group_count, me), ((group + group_count - 1) % group_count, me)]
    partners = [(group, partner_of(me, mask, member_count)) for mask in range(1, member_count)]
    everyone = ends + partners
    _, half, rows = share.shape
    classes = out.shape[0]
    block_count = rows // BR
    heights = (own_low.shape[1], own_high.shape[1])
    bands = (slice(0, heights[0]), slice(heights[0], half))
    twice = 2 * half - classes
    owns, keys = (own_low, own_high), (keys_low, keys_high)
    width = 2 * BR if block_count % 2 == 0 else BR
    in_chunk = width // BR
    chunks = rows // width
    near_at = rows + 2 * BR
    near = 4
    offsets = [(classes - half) * core, (classes - half) * (1 - core)]
    order = FIRST + tuple(range(PURE, cap))
    slots = tuple((link, s) for s in range(cap) for link in (0, 1))

    started = {}

    class Copy:
        def __init__(self, src, dst, sems, at, device):
            self.key = (id(sems), at)
            self.copy = pltpu.make_async_remote_copy(
                src_ref=src, dst_ref=dst, send_sem=sems.at[(0,) + at], recv_sem=sems.at[(1,) + at],
                device_id=device, device_id_type=MESH,
            )

        def start(self):
            started[self.key] = self
            self.copy.start()

        def wait_recv(self):
            self.copy.wait_recv()

        def wait_send(self):
            self.copy.wait_send()

    class Unit:
        def __init__(self, index, refs):
            self.index = index
            self.mine, self.oth, self.theirs, self.send, self.recv, self.fwd, self.near, self.far, self.far_in = refs

        def ex(self):
            return Copy(self.oth, self.theirs, ex_sem, (self.index,), sibling)

        def slot(self, link, s):
            i = link * cap + s
            return Copy(self.send.at[i], self.recv.at[i], slot_sem, (self.index, i), nexts[link])

        def forward(self, link, s):
            i = link * cap + s
            return Copy(self.recv.at[i], self.fwd.at[i], fwd_sem, (self.index, i), sibling)

        def sib(self, part):
            dst = self.recv if part == 1 else self.fwd
            return Copy(self.near.at[part], dst.at[2 * cap], near_sem, (self.index, part), sibling)

        def cross(self, i):
            return Copy(self.far.at[i], self.far_in.at[i], far_sem, (self.index, i), ends[i])

        def block_of(self, code):
            own = self.mine[jnp.minimum(code, block_count - 1)]
            return jnp.where(code < block_count, own, self.theirs[jnp.maximum(code - block_count, 0)])

    units = [Unit(i, unit_refs[9 * i:9 * i + 9]) for i in range(1 + 2 * ITERS)]
    emb = units[0]
    labels = [units[1 + 2 * stage:3 + 2 * stage] for stage in range(ITERS)]

    loads = [
        pltpu.make_async_copy(
            emb_hbm.at[:, :, pl.ds(pl.multiple_of(core * emb.oth.shape[2], 128), emb.oth.shape[2])],
            emb.mine, load_sem.at[0],
        ),
        pltpu.make_async_copy(
            emb_hbm.at[:, :, pl.ds(pl.multiple_of((1 - core) * emb.oth.shape[2], 128), emb.oth.shape[2])],
            emb.oth, load_sem.at[1],
        ),
        pltpu.make_async_copy(
            prior_hbm.at[pl.ds(pl.multiple_of(offsets[0], 8), half)], share.at[0], load_sem.at[2]
        ),
        pltpu.make_async_copy(
            prior_hbm.at[pl.ds(pl.multiple_of(offsets[1], 8), half)], share.at[1], load_sem.at[3]
        ),
        pltpu.make_async_copy(links_hbm, links, load_sem.at[4]),
        pltpu.make_async_copy(theirs_hbm, emb.theirs, load_sem.at[5]),
    ]
    barrier = pltpu.get_barrier_semaphore()
    for target in everyone:
        pl.semaphore_signal(barrier, inc=1, device_id=target, device_id_type=MESH)
    for i in (0, 5, 1, 2, 3, 4):
        loads[i].start()

    codes = [[(table[AT_CODES + link] >> (4 * s)) & 15 for s in range(cap)] for link in (0, 1)]
    relays = [table[AT_RELAYS + link] for link in (0, 1)]
    places = []
    for k in range(near):
        place = table[AT_PLACE + k]
        places.append(jnp.minimum(place % 8 + cap * (place // 8), 2 * cap))
    picks = [cross[0, ends[0][0]], cross[1, ends[1][0]]]
    picks += [table[AT_PICK + i] for i in range(member_count - 1)]
    sum_at = [table[AT_SUM + k] for k in range(near)]

    def side(unit):
        for part, ref in ((0, unit.mine), (1, unit.oth)):
            unit.near[part] = ref[picks[2]]
            unit.sib(part).start()
        for i in (0, 1):
            unit.far[i, 0] = unit.mine[picks[i]]
            unit.far[i, 1] = unit.oth[picks[i]]
            unit.cross(i).start()

    def first(unit):
        if unit is emb:
            for s in order:
                for link in (0, 1):
                    unit.send[link * cap + s] = unit.block_of(codes[link][s])
            pl.semaphore_wait(barrier, len(everyone))
        else:
            unit.ex().wait_recv()
        for s in order:
            for link in (0, 1):
                if unit is not emb:
                    unit.send[link * cap + s] = unit.block_of(codes[link][s])
                unit.slot(link, s).start()

    def relay(unit):
        for s in FIRST:
            for link in (0, 1):
                unit.slot(link, s).wait_recv()
        for s in FIRST:
            for link in (0, 1):
                passing = unit.recv[(1 - link) * cap + s]
                unit.send[link * cap + RELAY[s]] = jnp.where(
                    s < relays[link], passing, unit.block_of(codes[link][RELAY[s]])
                )
                unit.slot(link, RELAY[s]).start()
        for s in FIRST:
            for link in (0, 1):
                unit.forward(link, s).start()

    def pass_on(unit, which):
        for s in which:
            for link in (0, 1):
                unit.slot(link, s).wait_recv()
                unit.forward(link, s).start()

    pure = tuple(range(PURE, cap))

    def gathered(unit):
        for link, s in slots:
            unit.forward(link, s).wait_recv()
        for part in (0, 1):
            unit.sib(part).wait_recv()

    loads[0].wait()
    loads[5].wait()
    first(emb)
    loads[1].wait()
    side(emb)
    loads[2].wait()
    loads[3].wait()

    def lanes_of(c):
        return pl.ds(pl.multiple_of(c * width, width), width)

    def summed(value, part, t):
        if part == 0 or twice == 0:
            return jnp.sum(value, axis=0, keepdims=True)
        if t == 0:
            rest, again, count = value[twice:], value[:twice], core
        else:
            rest, again, count = value[:-twice], value[-twice:], 1 - core
        total = jnp.sum(rest, axis=0, keepdims=True)
        return total + jnp.sum(again, axis=0, keepdims=True) * count.astype(jnp.float32)

    def put_blocks(stage, part, t, c, value):
        unit = labels[stage][t]
        ref = unit.oth if part else unit.mine
        for b in range(in_chunk):
            ref[c * in_chunk + b] = value[:, b * BR:(b + 1) * BR]

    def first_labels(c, _):
        lanes = lanes_of(c)
        total = jnp.zeros((1, width), jnp.float32)
        for part in (0, 1):
            for t in (0, 1):
                total += summed(share[part, bands[t], lanes], part, t)
        scale = 1.0 / total
        for part in (0, 1):
            for t in (0, 1):
                value = share[part, bands[t], lanes] * scale
                share[part, bands[t], lanes] = value
                value = value.astype(jnp.bfloat16)
                owns[t][part, :, lanes] = value
                put_blocks(0, part, t, c, value)
        return _

    lax.fori_loop(0, chunks, first_labels, 0)
    for t in (0, 1):
        labels[0][t].ex().start()
        side(labels[0][t])

    features = 2 * emb.oth.shape[2]

    def score_rows(at, low, high, finish):
        height = low.shape[0]

        def body(c, _):
            lanes = lanes_of(c)
            picked = pl.ds(c * in_chunk, in_chunk)
            value = sum(
                lax.dot_general(
                    keys, ref[picked].reshape(width, features // 2), (((1,), (1,)), ((), ())),
                    preferred_element_type=jnp.float32,
                )
                for keys, ref in ((low[...], emb.mine), (high[...], emb.oth))
            )
            scores[at:at + height, lanes] = finish(value * features ** (-0.5), c, lanes)
            return _

        lax.fori_loop(0, chunks, body, 0)

    def off_diagonal(value, c, lanes):
        key_ids = lax.broadcasted_iota(jnp.int32, (rows, width), 0)
        row_ids = lax.broadcasted_iota(jnp.int32, (rows, width), 1) + c * width
        return jnp.where(key_ids != row_ids, value, -jnp.inf)

    def linked(names):
        def finish(value, c, lanes):
            parts = []
            for i, name in enumerate(names):
                bias = jnp.max(jnp.where(links[:, lanes] == name, 0.0, -jnp.inf), axis=0, keepdims=True)
                parts.append(value[i * BR:(i + 1) * BR] + bias)
            return jnp.concatenate(parts, axis=0)

        return finish

    for b in range(block_count):
        key_emb[0, b * BR:(b + 1) * BR] = emb.mine[b]
        key_emb[1, b * BR:(b + 1) * BR] = emb.oth[b]
    score_rows(0, key_emb.at[0], key_emb.at[1], off_diagonal)
    loads[4].wait()

    relay(emb)
    pass_on(emb, pure)
    first(labels[0][0])
    for i in (0, 1):
        emb.cross(i).wait_recv()
        for part in (0, 1):
            key_emb[part, i * BR:(i + 1) * BR] = emb.far_in[i, part]
    low, high = (key_emb.at[part, pl.ds(0, 2 * BR)] for part in (0, 1))
    score_rows(rows, low, high, linked((near, near + 1)))
    pass_on(emb, RELAY)
    gathered(emb)
    for k in range(near):
        for part, ref in ((0, emb.recv), (1, emb.fwd)):
            key_emb[part, k * BR:(k + 1) * BR] = ref[places[k]]
    relay(labels[0][0])
    first(labels[0][1])
    low, high = (key_emb.at[part, pl.ds(0, near * BR)] for part in (0, 1))
    score_rows(near_at, low, high, linked(range(near)))

    def soften(b, _):
        lanes = pl.ds(pl.multiple_of(b * BR, BR), BR)
        value = scores[:, lanes]
        powers = jnp.exp(value - jnp.max(value, axis=0, keepdims=True))
        total = jnp.sum(powers, axis=0, keepdims=True)
        weights[:, lanes] = (powers * (1.0 / total)).astype(jnp.bfloat16)
        return _

    lax.fori_loop(0, block_count, soften, 0)

    def scaled(block, at):
        return (block.astype(jnp.float32) * (1.0 / sum_recv[at][:1])).astype(jnp.bfloat16)

    def premix(stage, t):
        unit = labels[stage][t]
        for i in (0, 1):
            unit.cross(i).wait_recv()
            for part in (0, 1):
                block = unit.far_in[i, part]
                owns[t][part, :, rows + i * BR:rows + (i + 1) * BR] = scaled(block, i) if stage else block

        def body(c, _):
            lanes = lanes_of(c)
            for part in (0, 1):
                mix[part, bands[t], lanes] = jnp.dot(
                    owns[t][part], weights[:near_at, lanes], preferred_element_type=jnp.float32
                )
            return _

        lax.fori_loop(0, chunks, body, 0)

    def neighbour_mix(stage, t, finish):
        unit = labels[stage][t]
        gathered(unit)
        for k in range(near):
            for part, ref in ((0, unit.recv), (1, unit.fwd)):
                block = ref[places[k]]
                keys[t][part, :, k * BR:(k + 1) * BR] = scaled(block, sum_at[k]) if stage else block

        def body(c, _):
            lanes = lanes_of(c)
            total_sum = jnp.zeros((1, width), jnp.float32)
            for part in (0, 1):
                total = mix[part, bands[t], lanes] + jnp.dot(
                    keys[t][part], weights[near_at:, lanes], preferred_element_type=jnp.float32
                )
                mixed = MIXING * total + (1.0 - MIXING) * share[part, bands[t], lanes]
                squared = mixed * mixed
                total_sum += summed(squared, part, t)
                finish(c, lanes, part, squared)
            for b in range(in_chunk):
                value = jnp.broadcast_to(total_sum[:, b * BR:(b + 1) * BR], (8, BR))
                at = c * in_chunk + b
                sums[at] = value if t == 0 else sums[at] + value
            return _

        lax.fori_loop(0, chunks, body, 0)

    def middle(stage, t):
        def finish(c, lanes, part, squared):
            mix[part, bands[t], lanes] = squared
            put_blocks(stage + 1, part, t, c, squared.astype(jnp.bfloat16))

        return finish

    def last(t):
        def finish(c, lanes, part, squared):
            begin = pl.multiple_of(offsets[part] + bands[t].start, 8)
            out[pl.ds(begin, heights[t]), lanes] = squared

        return finish

    def sum_copy(s):
        return Copy(sum_send.at[s], sum_recv.at[s], sum_sem, (s,), everyone[s])

    def own_labels(c, _):
        lanes = lanes_of(c)
        parts = [sums[c * in_chunk + b][:1] for b in range(in_chunk)]
        scale = 1.0 / jnp.concatenate(parts, axis=1)
        for part in (0, 1):
            for t in (0, 1):
                owns[t][part, :, lanes] = (mix[part, bands[t], lanes] * scale).astype(jnp.bfloat16)
        return _

    for stage in range(ITERS):
        final = stage == ITERS - 1
        this = labels[stage]
        premix(stage, 0)
        pass_on(this[0], pure + RELAY)
        relay(this[1])
        neighbour_mix(stage, 0, last(0) if final else middle(stage, 0))
        if not final:
            later = labels[stage + 1]
            later[0].ex().start()
            side(later[0])
        premix(stage, 1)
        if not final:
            first(later[0])
        pass_on(this[1], pure + RELAY)
        neighbour_mix(stage, 1, last(1) if final else middle(stage, 1))
        if not final:
            for s in range(len(everyone)):
                sum_send[s] = sums[picks[s]]
                sum_copy(s).start()
            later[1].ex().start()
            side(later[1])
            relay(later[0])
            first(later[1])
            lax.fori_loop(0, chunks, own_labels, 0)
            for s in range(len(everyone)):
                sum_copy(s).wait_recv()

    for b in range(block_count):
        row_sums[:, b * BR:(b + 1) * BR] = sums[b]
    for copy in started.values():
        copy.wait_send()


def spread(cap, member_count, group_count, table, cross, emb, theirs, prior, links):
    block_count, _, features = emb.shape
    classes, rows = prior.shape
    half, heights = halves_of(classes)
    any_space = pl.BlockSpec(memory_space=pl.ANY)
    smem = pl.BlockSpec(memory_space=pltpu.SMEM)
    vmem = pl.BlockSpec(memory_space=pltpu.VMEM)
    bf16, f32 = jnp.bfloat16, jnp.float32
    keys = rows + 6 * BR
    partners = member_count + 1

    def unit(height, wide):
        counts = (
            (block_count,), (block_count,), (block_count,), (2 * cap,), (2 * cap + 1,), (2 * cap + 1,), (2,), (2, 2), (2, 2)
        )
        return [pltpu.VMEM(count + (height, wide), bf16) for count in counts]

    def dma(*shape):
        return pltpu.SemaphoreType.DMA((2,) + shape)

    units = 1 + 2 * ITERS
    return pl.pallas_call(
        functools.partial(spread_kernel, cap, member_count, group_count),
        out_shape=(pltpu.VMEM((classes, rows), f32), pltpu.VMEM((8, rows), f32)),
        in_specs=[smem] * 2 + [any_space] * 4,
        out_specs=(vmem, vmem),
        scratch_shapes=[
            pltpu.VMEM((2, half, rows), f32),
            pltpu.VMEM((links.shape[0], rows), jnp.int32),
            pltpu.VMEM((keys, rows), f32),
            pltpu.VMEM((keys, rows), bf16),
            pltpu.VMEM((2, half, rows), f32),
            pltpu.VMEM((block_count, 8, BR), f32),
            pltpu.VMEM((partners, 8, BR), f32),
            pltpu.VMEM((partners, 8, BR), f32),
            pltpu.VMEM((2, heights[0], rows + 2 * BR), bf16),
            pltpu.VMEM((2, heights[1], rows + 2 * BR), bf16),
            pltpu.VMEM((2, heights[0], 4 * BR), bf16),
            pltpu.VMEM((2, heights[1], 4 * BR), bf16),
            pltpu.VMEM((2, rows, features // 2), bf16),
            *unit(BR, features // 2),
            *(ref for _ in range(ITERS) for height in heights for ref in unit(height, BR)),
            pltpu.SemaphoreType.DMA((6,)),
            dma(units), dma(units, 2 * cap), dma(units, 2 * cap), dma(units, 2), dma(units, 2), dma(partners),
        ],
        compiler_params=pltpu.CompilerParams(
            collective_id=cap, has_side_effects=True, vmem_limit_bytes=60 * 2**20
        ),
    )(table, cross, emb, theirs, prior, links)


def spread_body(embeddings, prior, source_member, source_block, cross_block, row_links):
    member_count = lax.axis_size("member")
    group_count = lax.axis_size("group")
    rows, features = embeddings.shape
    emb_blocks = embeddings.reshape(rows // BR, BR, features)
    table, theirs = route(source_member[0].T, source_block[0].T, emb_blocks, group_count)
    caps = (5, 6, 7, 8)
    branches = [functools.partial(spread, cap, member_count, group_count) for cap in caps]
    squared, sums = lax.switch(
        jnp.clip(table[0] - caps[0], 0, len(caps) - 1), branches,
        table, cross_block[:, 0, :].T, emb_blocks, theirs, prior.T, row_links.T,
    )
    return (squared * (prior.shape[1] / sums[:1])).T


def solution(mesh):
    spread_fits = mesh.shape["member"] == 8
    body = spread_body if spread_fits else relay_body
    placed = (
        P(("group", "member"), None),
        P(("group", "member"), None),
        P("group", None, None),
        P("group", None, None),
        P(None, "member", None),
        P(("group", "member"), None),
    )
    return jax.shard_map(
        body, mesh=mesh, in_specs=placed, out_specs=P(("group", "member"), None), check_vma=False
    )
```

```python
import functools

import jax
import jax.numpy as jnp
from jax import lax
from jax.experimental import pallas as pl
from jax.experimental.pallas import tpu as pltpu
from jax.sharding import PartitionSpec as P

BR = 128
SERVE_CAP = 7
ITERS = 2


MIXING = 0.8


def extended(value, sides, width):
    for axis, dim in sides:
        size, length = (lax.axis_size(axis), value.shape[dim])
        up = [(i, (i + 1) % size) for i in range(size)]
        down = [(j, i) for i, j in up]
        last = lax.slice_in_dim(value, length - width, length, axis=dim)
        first = lax.slice_in_dim(value, 0, width, axis=dim)
        before = lax.ppermute(last, axis, up)
        after = lax.ppermute(first, axis, down)
        value = jnp.concatenate([before, value, after], axis=dim)
    return value


def allowed_mask(row_links, near_total, slot_total, row_count, block_rows):
    slot_ids = jnp.arange(slot_total, dtype=jnp.int32)
    slot_hits = jnp.any(row_links[:, :, None] == slot_ids[None, None, :], axis=1)
    near_mask = jnp.tile(slot_hits[:, :near_total], (1, block_rows))
    far_mask = jnp.repeat(slot_hits[:, near_total:], block_rows, axis=1)
    row_ids = lax.broadcasted_iota(jnp.int32, (row_count, row_count), 0)
    col_ids = lax.broadcasted_iota(jnp.int32, (row_count, row_count), 1)
    local_mask = row_ids != col_ids
    return jnp.concatenate([local_mask, near_mask, far_mask], axis=1)


def kernel_weights(queries, key_rows, allowed):
    features = queries.shape[1]
    scores = lax.dot_general(
        queries, key_rows, (((1,), (1,)), ((), ())), preferred_element_type=jnp.float32
    )
    scores = scores * features ** (-0.5)
    scores = jnp.where(allowed, scores, -jnp.inf)
    highest = jnp.max(scores, axis=1, keepdims=True)
    powers = jnp.where(allowed, jnp.exp(scores - highest), 0.0)
    return (powers / jnp.sum(powers, axis=1, keepdims=True)).astype(jnp.bfloat16)


def sharpen(weights, key_labels, prior_share):
    mixed = (
        MIXING * jnp.dot(weights, key_labels, preferred_element_type=jnp.float32)
        + (1.0 - MIXING) * prior_share
    )
    squared = mixed * mixed
    return squared / jnp.sum(squared, axis=1, keepdims=True)


def one_hot(ids, count):
    return (ids[..., None] == jnp.arange(count, dtype=jnp.int32)).astype(jnp.bfloat16)


def near_keys(delivered):
    return delivered.reshape(-1, delivered.shape[-1])


def far_keys(padded):
    return jnp.concatenate([padded[0], padded[-1]], axis=0)


def relay_body(embeddings, prior, source_member, source_block, cross_block, row_links):
    member_count = lax.axis_size("member")
    group_count = lax.axis_size("group")
    group_index = lax.axis_index("group")
    member_index = lax.axis_index("member")
    row_count, features = embeddings.shape
    classes = prior.shape[1]
    block_rows = BR
    block_count = row_count // block_rows
    piece_rows = block_rows // member_count
    owners = source_member[0]
    slot_count = owners.shape[1]
    flat_owner = owners.reshape(-1)
    flat_block = source_block[0].reshape(-1)
    order_ids = jnp.arange(flat_owner.shape[0], dtype=jnp.int32)
    earlier = (flat_owner[:, None] == flat_owner[None, :]) & (
        order_ids[None, :] < order_ids[:, None]
    )
    rank_ids = jnp.sum(earlier.astype(jnp.int32), axis=1)
    serve_ids = jnp.arange(SERVE_CAP, dtype=jnp.int32)
    serving = (flat_owner[None, :] == member_index) & (rank_ids[None, :] == serve_ids[:, None])
    served_blocks = jnp.sum(jnp.where(serving, flat_block[None, :], 0), axis=1)
    served_hot = one_hot(served_blocks, block_count)
    rank_grid = rank_ids.reshape(member_count, slot_count)
    deliver_hot = one_hot(owners, member_count)[..., :, None] * one_hot(rank_grid, SERVE_CAP)[..., None, :]
    below_group = (group_index + group_count - 1) % group_count
    above_group = (group_index + 1) % group_count
    group_ids = jnp.arange(group_count, dtype=jnp.int32)
    cross_pick = jnp.stack([
        jnp.sum(jnp.where(group_ids == below_group, cross_block[:, 0, 1], 0)),
        jnp.sum(jnp.where(group_ids == above_group, cross_block[:, 0, 0], 0)),
    ])
    cross_hot = one_hot(cross_pick, block_count)
    allowed = allowed_mask(
        row_links, slot_count, slot_count + cross_block.shape[2], row_count, block_rows
    )
    prior_share = prior / jnp.sum(prior, axis=1, keepdims=True)
    labels = prior_share.astype(jnp.bfloat16)
    emb_blocks = embeddings.reshape(block_count, block_rows, features)

    def cross_of(blocks):
        return jnp.einsum("cb,brl->crl", cross_hot, blocks, preferred_element_type=jnp.float32).astype(jnp.bfloat16)

    def relay_pieces(flat_rows):
        blocks = flat_rows.reshape(block_count, member_count, piece_rows, flat_rows.shape[-1])
        return jnp.einsum("sb,bmpl->mpsl", served_hot, blocks, preferred_element_type=jnp.float32).astype(jnp.bfloat16)

    def deliver_pieces(received):
        return jnp.einsum("mkos,opsl->mpkl", deliver_hot, received, preferred_element_type=jnp.float32).astype(jnp.bfloat16)

    result = prior_share
    emb_relay = lax.all_to_all(
        relay_pieces(embeddings), "member", split_axis=0, concat_axis=0, tiled=True
    )
    emb_near = lax.all_to_all(
        deliver_pieces(emb_relay), "member", split_axis=0, concat_axis=0, tiled=True
    )
    emb_far = extended(cross_of(emb_blocks), (("group", 0),), 1)
    key_rows = jnp.concatenate([embeddings, near_keys(emb_near), far_keys(emb_far)], axis=0)
    weights = kernel_weights(embeddings, key_rows, allowed)
    for iteration in range(ITERS):
        lab_blocks = labels.reshape(block_count, block_rows, classes)
        lab_relay = lax.all_to_all(
            relay_pieces(labels), "member", split_axis=0, concat_axis=0, tiled=True
        )
        lab_near = lax.all_to_all(
            deliver_pieces(lab_relay), "member", split_axis=0, concat_axis=0, tiled=True
        )
        lab_far = extended(cross_of(lab_blocks), (("group", 0),), 1)
        key_labels = jnp.concatenate([labels, near_keys(lab_near), far_keys(lab_far)], axis=0)
        result = sharpen(weights, key_labels, prior_share)
        labels = result.astype(jnp.bfloat16)
    return result * classes


MESH = pl.DeviceIdType.MESH
TABLE = 32
AT_CODES, AT_RELAYS, AT_PLACE, AT_SUM, AT_PICK = 1, 3, 5, 13, 17
FIRST, RELAY, PURE = (0, 1), (2, 3), 4
LINKS_OUT = ((0, 1), (1, 2))


def partner_of(member, mask, member_count):
    bit = 1
    while bit < member_count:
        if mask & bit:
            member = member + bit - 2 * bit * (member // bit % 2)
        bit *= 2
    return member


def same(left, right):
    gap = left - right
    return 1 - jnp.minimum(gap * gap, 1)


def pairs_in(bits):
    return bits - (bits >> 1)


def route_kernel(
    group_count, block_count, owners, blocks, emb_hbm, table, theirs, mine, others, send_sem, recv_sem, swap_sem
):
    group = lax.axis_index("group")
    me = lax.axis_index("member")
    core = me % 2
    in_slots, members = owners.shape
    targets = [((group + i) % group_count, me) for i in range(1, group_count)]
    sibling = (group, partner_of(me, 1, members))
    barrier = pltpu.get_barrier_semaphore()
    for target in targets + [sibling]:
        pl.semaphore_signal(barrier, inc=1, device_id=target, device_id_type=MESH)

    def named_of(p):
        bits = jnp.int32(0)
        for k in range(in_slots):
            bits += jnp.left_shift(jnp.int32(1), owners[k, p])
        return bits

    named = [named_of(p) for p in range(members)]

    def flow(src, dst):
        return sum(pairs_in((named[2 * dst + t] >> (2 * src)) & 3) for t in (0, 1))

    chips = range(members // 2)
    flat = [[flow(c, c ^ 1), flow(c, c ^ 2)] for c in chips]
    cornered = [flow(c, c ^ 3) for c in chips]
    choice = lax.broadcasted_iota(jnp.int32, (8, 128), 0) * 128 + lax.broadcasted_iota(jnp.int32, (8, 128), 1)
    choice = choice & 255
    turn = [(choice >> (2 * c)) & 3 for c in chips]
    fits = choice >= 0
    for c in chips:
        fits &= (turn[c] <= 2) & (turn[c] <= cornered[c]) & (turn[c] >= cornered[c] - 2)

    def best_of(half):
        load = jnp.zeros_like(choice)
        for c in chips:
            spare = 1 - (c // 2 + c % 2 + half) % 2
            load = jnp.maximum(load, 2 * (turn[c] - turn[c ^ 2]) + (2 * (flat[c][0] + cornered[c ^ 2]) - spare))
            load = jnp.maximum(load, 2 * (turn[c ^ 1] - turn[c]) + (2 * (flat[c][1] + cornered[c]) - spare))
        return jnp.min(jnp.where(fits, load * 256 + choice, 1 << 20))

    best = [best_of(half) for half in (0, 1)]
    need = jnp.maximum(best[0] >> 8, best[1] >> 8)
    turns = [best[0] + (best[1] - best[0]) * core, best[1] + (best[0] - best[1]) * core]

    mine[...] = jnp.full(mine.shape, need, jnp.int32)
    pl.semaphore_wait(barrier, len(targets) + 1)
    copies = []
    for i, target in enumerate(targets):
        copy = pltpu.make_async_remote_copy(
            src_ref=mine, dst_ref=others.at[i], send_sem=send_sem.at[i], recv_sem=recv_sem.at[i],
            device_id=target, device_id_type=MESH,
        )
        copy.start()
        copies.append(copy)

    half = theirs.shape[2]
    swap = pltpu.make_async_remote_copy(
        src_ref=emb_hbm.at[:, :, pl.ds(pl.multiple_of((1 - core) * half, 128), half)], dst_ref=theirs,
        send_sem=swap_sem.at[0], recv_sem=swap_sem.at[1], device_id=sibling, device_id_type=MESH,
    )
    swap.start()

    packed_corner = sum(cornered[c] << (4 * c) for c in chips)
    chip = [partner_of(me, 2 * e, members) // 2 for e in range(4)]
    bits = [[named_of(2 * chip[e] + t) for t in (0, 1)] for e in range(4)]

    def corner_of(c):
        return (packed_corner >> (4 * c)) & 15

    def turn_of(c, part):
        return (turns[part] >> (2 * c)) & 3

    def hop(e, link, part):
        if link == 0:
            return turn_of(chip[e], part), corner_of(chip[e ^ 2]) - turn_of(chip[e ^ 2], part)
        return corner_of(chip[e]) - turn_of(chip[e], part), turn_of(chip[e ^ 1], part)

    def flag(src, s, dst, t):
        return (bits[dst][t] >> (2 * chip[src] + s)) & 1

    def pick(src, dst):
        total = jnp.int32(0)
        for k in range(in_slots):
            total += same(owners[k, dst], src) * blocks[k, dst]
        return total

    def placed(at, relays):
        return jnp.minimum(at + jnp.where(at >= 2, relays, 0), 7)

    codes = [jnp.int32(0), jnp.int32(0)]

    def code_of(s, e, t):
        apart = core + s - 2 * core * s
        return pick(2 * chip[0] + s, 2 * chip[e] + t) + block_count * apart

    for link, e in LINKS_OUT:
        at, relays = hop(0, link, 0)
        table[AT_RELAYS + link] = relays
        for t in (0, 1):
            for s in (0, 1):
                there = flag(0, s, e, t)
                codes[link] += there * jnp.left_shift(code_of(s, e, t), 4 * placed(at, relays))
                at += there
    at = jnp.int32(0)
    for t in (0, 1):
        for s in (0, 1):
            there = flag(0, s, 3, t)
            code = code_of(s, 3, t)
            split = turn_of(chip[0], 0)
            early = jnp.where(at < split, there, 0)
            codes[0] += early * jnp.left_shift(code, 4 * jnp.minimum(at, 7))
            codes[1] += (there - early) * jnp.left_shift(code, 4 * jnp.maximum(at - split, 0))
            at += there
    for link in (0, 1):
        table[AT_CODES + link] = codes[link]

    wanted = [owners[k, me] for k in range(in_slots)]
    places = [[same(q, partner_of(me, 1, members)) * 16 for q in wanted] for _ in (0, 1)]
    for e in (1, 2, 3):
        flags = [[flag(e, s, 0, t) for s in (0, 1)] for t in (0, 1)]
        for s in (0, 1):
            ahead = core * (flags[0][0] + flags[0][1])
            if s == 1:
                ahead += jnp.where(core == 0, flags[0][0], flags[1][0])
            named_here = [same(q, 2 * chip[e] + s) for q in wanted]
            for part in (0, 1):
                if e < 3:
                    link = e - 1
                    begin, relays = hop(e, link, part)
                    place = 8 * link + placed(begin + ahead, relays)
                else:
                    split = turn_of(chip[3], part)
                    place = jnp.where(ahead < split, 8 + RELAY[0] + ahead, RELAY[0] + ahead - split)
                for k in range(in_slots):
                    places[part][k] += named_here[k] * place
    for k in range(in_slots):
        for part in (0, 1):
            table[AT_PLACE + part * in_slots + k] = places[part][k]
        index = jnp.int32(0)
        for mask in range(1, members):
            index += same(wanted[k], partner_of(me, mask, members)) * (mask + 1)
        table[AT_SUM + k] = index
    for mask in range(1, members):
        table[AT_PICK + mask - 1] = pick(me, partner_of(me, mask, members))
    for i in range(AT_PICK + members - 1, TABLE):
        table[i] = jnp.int32(0)

    most = mine[...]
    for i, copy in enumerate(copies):
        copy.wait()
        most = jnp.maximum(most, others[i])
    table[0] = jnp.max(most)
    swap.wait()


def route(owners, blocks, emb, group_count):
    smem = pl.BlockSpec(memory_space=pltpu.SMEM)
    any_space = pl.BlockSpec(memory_space=pl.ANY)
    block_count, block_rows, features = emb.shape
    others = max(group_count - 1, 1)
    return pl.pallas_call(
        functools.partial(route_kernel, group_count, block_count),
        out_shape=(
            jax.ShapeDtypeStruct((TABLE,), jnp.int32),
            jax.ShapeDtypeStruct((block_count, block_rows, features // 2), emb.dtype),
        ),
        in_specs=[smem] * 2 + [any_space],
        out_specs=(smem, any_space),
        scratch_shapes=[
            pltpu.VMEM((8, 128), jnp.int32),
            pltpu.VMEM((others, 8, 128), jnp.int32),
            pltpu.SemaphoreType.DMA((others,)),
            pltpu.SemaphoreType.DMA((others,)),
            pltpu.SemaphoreType.DMA((2,)),
        ],
        compiler_params=pltpu.CompilerParams(collective_id=0, has_side_effects=True),
    )(owners, blocks, emb)


def halves_of(classes):
    half = -(-classes // 16) * 8
    low = -(-half // 32) * 16
    return half, (low, half - low)


def spread_kernel(
    cap, uneven, member_count, group_count,
    table, cross, emb_hbm, theirs_hbm, prior_hbm, links_hbm, out, row_sums,
    share, links, scores, weights, mix, sums, sum_send, sum_recv,
    own_low, own_high, keys_low, keys_high, key_emb, *rest,
):
    unit_refs, (load_sem, ex_sem, slot_sem, fwd_sem, near_sem, far_sem, sum_sem) = rest[:-7], rest[-7:]
    group = lax.axis_index("group")
    me = lax.axis_index("member")
    core = me % 2
    sibling = (group, partner_of(me, 1, member_count))
    nexts = [(group, partner_of(me, 2, member_count)), (group, partner_of(me, 4, member_count))]
    ends = [((group + 1) % group_count, me), ((group + group_count - 1) % group_count, me)]
    partners = [(group, partner_of(me, mask, member_count)) for mask in range(1, member_count)]
    everyone = ends + partners
    _, half, rows = share.shape
    classes = out.shape[0]
    block_count = rows // BR
    heights = (own_low.shape[1], own_high.shape[1])
    bands = (slice(0, heights[0]), slice(heights[0], half))
    twice = 2 * half - classes
    owns, keys = (own_low, own_high), (keys_low, keys_high)
    width = 2 * BR if block_count % 2 == 0 else BR
    in_chunk = width // BR
    chunks = rows // width
    near_at = rows + 2 * BR
    near = 4
    offsets = [(classes - half) * core, (classes - half) * (1 - core)]
    order = FIRST + tuple(range(PURE, cap))
    slots = tuple((link, s) for s in range(cap) for link in (0, 1))

    started = {}
    parity = (me // 4 + me // 2 + me) % 2

    def only(which, act):
        if which is None:
            act()
        else:
            pl.when(parity == which)(act)

    class Copy:
        def __init__(self, src, dst, sems, at, device, sender=None):
            self.key = (id(sems), at)
            self.sender = sender
            self.taker = None if sender is None else 1 - sender
            self.copy = pltpu.make_async_remote_copy(
                src_ref=src, dst_ref=dst, send_sem=sems.at[(0,) + at], recv_sem=sems.at[(1,) + at],
                device_id=device, device_id_type=MESH,
            )

        def start(self):
            started[self.key] = self
            only(self.sender, self.copy.start)

        def wait_recv(self):
            only(self.taker, self.copy.wait_recv)

        def wait_send(self):
            only(self.sender, self.copy.wait_send)

    def spare(s, which):
        return which if uneven and s == cap - 1 else None

    class Unit:
        def __init__(self, index, refs):
            self.index = index
            self.mine, self.oth, self.theirs, self.send, self.recv, self.fwd, self.near, self.far, self.far_in = refs

        def ex(self):
            return Copy(self.oth, self.theirs, ex_sem, (self.index,), sibling)

        def slot(self, link, s):
            i = link * cap + s
            return Copy(self.send.at[i], self.recv.at[i], slot_sem, (self.index, i), nexts[link], spare(s, 0))

        def forward(self, link, s):
            i = link * cap + s
            return Copy(self.recv.at[i], self.fwd.at[i], fwd_sem, (self.index, i), sibling, spare(s, 1))

        def sib(self, part):
            dst = self.recv if part == 1 else self.fwd
            return Copy(self.near.at[part], dst.at[2 * cap], near_sem, (self.index, part), sibling)

        def cross(self, i):
            return Copy(self.far.at[i], self.far_in.at[i], far_sem, (self.index, i), ends[i])

        def block_of(self, code):
            own = self.mine[jnp.minimum(code, block_count - 1)]
            return jnp.where(code < block_count, own, self.theirs[jnp.maximum(code - block_count, 0)])

    units = [Unit(i, unit_refs[9 * i:9 * i + 9]) for i in range(1 + 2 * ITERS)]
    emb = units[0]
    labels = [units[1 + 2 * stage:3 + 2 * stage] for stage in range(ITERS)]

    loads = [
        pltpu.make_async_copy(
            emb_hbm.at[:, :, pl.ds(pl.multiple_of(core * emb.oth.shape[2], 128), emb.oth.shape[2])],
            emb.mine, load_sem.at[0],
        ),
        pltpu.make_async_copy(
            emb_hbm.at[:, :, pl.ds(pl.multiple_of((1 - core) * emb.oth.shape[2], 128), emb.oth.shape[2])],
            emb.oth, load_sem.at[1],
        ),
        pltpu.make_async_copy(
            prior_hbm.at[pl.ds(pl.multiple_of(offsets[0], 8), half)], share.at[0], load_sem.at[2]
        ),
        pltpu.make_async_copy(
            prior_hbm.at[pl.ds(pl.multiple_of(offsets[1], 8), half)], share.at[1], load_sem.at[3]
        ),
        pltpu.make_async_copy(links_hbm, links, load_sem.at[4]),
        pltpu.make_async_copy(theirs_hbm, emb.theirs, load_sem.at[5]),
    ]
    barrier = pltpu.get_barrier_semaphore()
    for target in everyone:
        pl.semaphore_signal(barrier, inc=1, device_id=target, device_id_type=MESH)
    for i in (0, 5, 1, 2, 3, 4):
        loads[i].start()

    codes = [[(table[AT_CODES + link] >> (4 * s)) & 15 for s in range(cap)] for link in (0, 1)]
    relays = [table[AT_RELAYS + link] for link in (0, 1)]
    places = []
    for part in (0, 1):
        at = [table[AT_PLACE + part * near + k] for k in range(near)]
        places.append([jnp.minimum(place % 8 + cap * (place // 8), 2 * cap) for place in at])
    picks = [cross[0, ends[0][0]], cross[1, ends[1][0]]]
    picks += [table[AT_PICK + i] for i in range(member_count - 1)]
    sum_at = [table[AT_SUM + k] for k in range(near)]

    def side(unit):
        for part, ref in ((0, unit.mine), (1, unit.oth)):
            unit.near[part] = ref[picks[2]]
            unit.sib(part).start()
        for i in (0, 1):
            unit.far[i, 0] = unit.mine[picks[i]]
            unit.far[i, 1] = unit.oth[picks[i]]
            unit.cross(i).start()

    def first(unit):
        if unit is emb:
            for s in order:
                for link in (0, 1):
                    unit.send[link * cap + s] = unit.block_of(codes[link][s])
            pl.semaphore_wait(barrier, len(everyone))
        else:
            unit.ex().wait_recv()
        for s in order:
            for link in (0, 1):
                if unit is not emb:
                    unit.send[link * cap + s] = unit.block_of(codes[link][s])
                unit.slot(link, s).start()

    def relay(unit):
        for s in FIRST:
            for link in (0, 1):
                unit.slot(link, s).wait_recv()
        for s in FIRST:
            for link in (0, 1):
                passing = unit.recv[(1 - link) * cap + s]
                unit.send[link * cap + RELAY[s]] = jnp.where(
                    s < relays[link], passing, unit.block_of(codes[link][RELAY[s]])
                )
                unit.slot(link, RELAY[s]).start()
        for s in FIRST:
            for link in (0, 1):
                unit.forward(link, s).start()

    def pass_on(unit, which):
        for s in which:
            for link in (0, 1):
                unit.slot(link, s).wait_recv()
                unit.forward(link, s).start()

    pure = tuple(range(PURE, cap))

    def gathered(unit):
        for link, s in slots:
            unit.forward(link, s).wait_recv()
        for part in (0, 1):
            unit.sib(part).wait_recv()

    loads[0].wait()
    loads[5].wait()
    first(emb)
    loads[1].wait()
    side(emb)
    loads[2].wait()
    loads[3].wait()

    def lanes_of(c):
        return pl.ds(pl.multiple_of(c * width, width), width)

    def summed(value, part, t):
        if part == 0 or twice == 0:
            return jnp.sum(value, axis=0, keepdims=True)
        if t == 0:
            rest, again, count = value[twice:], value[:twice], core
        else:
            rest, again, count = value[:-twice], value[-twice:], 1 - core
        total = jnp.sum(rest, axis=0, keepdims=True)
        return total + jnp.sum(again, axis=0, keepdims=True) * count.astype(jnp.float32)

    def put_blocks(stage, part, t, c, value):
        unit = labels[stage][t]
        ref = unit.oth if part else unit.mine
        for b in range(in_chunk):
            ref[c * in_chunk + b] = value[:, b * BR:(b + 1) * BR]

    def first_labels(c, _):
        lanes = lanes_of(c)
        total = jnp.zeros((1, width), jnp.float32)
        for part in (0, 1):
            for t in (0, 1):
                total += summed(share[part, bands[t], lanes], part, t)
        scale = 1.0 / total
        for part in (0, 1):
            for t in (0, 1):
                value = share[part, bands[t], lanes] * scale
                share[part, bands[t], lanes] = value
                value = value.astype(jnp.bfloat16)
                owns[t][part, :, lanes] = value
                put_blocks(0, part, t, c, value)
        return _

    lax.fori_loop(0, chunks, first_labels, 0)
    for t in (0, 1):
        labels[0][t].ex().start()
        side(labels[0][t])

    features = 2 * emb.oth.shape[2]

    def score_rows(at, low, high, finish):
        height = low.shape[0]

        def body(c, _):
            lanes = lanes_of(c)
            picked = pl.ds(c * in_chunk, in_chunk)
            value = sum(
                lax.dot_general(
                    keys, ref[picked].reshape(width, features // 2), (((1,), (1,)), ((), ())),
                    preferred_element_type=jnp.float32,
                )
                for keys, ref in ((low[...], emb.mine), (high[...], emb.oth))
            )
            scores[at:at + height, lanes] = finish(value * features ** (-0.5), c, lanes)
            return _

        lax.fori_loop(0, chunks, body, 0)

    def off_diagonal(value, c, lanes):
        key_ids = lax.broadcasted_iota(jnp.int32, (rows, width), 0)
        row_ids = lax.broadcasted_iota(jnp.int32, (rows, width), 1) + c * width
        return jnp.where(key_ids != row_ids, value, -jnp.inf)

    def linked(names):
        def finish(value, c, lanes):
            parts = []
            for i, name in enumerate(names):
                bias = jnp.max(jnp.where(links[:, lanes] == name, 0.0, -jnp.inf), axis=0, keepdims=True)
                parts.append(value[i * BR:(i + 1) * BR] + bias)
            return jnp.concatenate(parts, axis=0)

        return finish

    for b in range(block_count):
        key_emb[0, b * BR:(b + 1) * BR] = emb.mine[b]
        key_emb[1, b * BR:(b + 1) * BR] = emb.oth[b]
    score_rows(0, key_emb.at[0], key_emb.at[1], off_diagonal)
    loads[4].wait()

    relay(emb)
    pass_on(emb, pure)
    first(labels[0][0])
    for i in (0, 1):
        emb.cross(i).wait_recv()
        for part in (0, 1):
            key_emb[part, i * BR:(i + 1) * BR] = emb.far_in[i, part]
    low, high = (key_emb.at[part, pl.ds(0, 2 * BR)] for part in (0, 1))
    score_rows(rows, low, high, linked((near, near + 1)))
    pass_on(emb, RELAY)
    gathered(emb)
    for k in range(near):
        for part, ref in ((0, emb.recv), (1, emb.fwd)):
            key_emb[part, k * BR:(k + 1) * BR] = ref[places[part][k]]
    relay(labels[0][0])
    first(labels[0][1])
    low, high = (key_emb.at[part, pl.ds(0, near * BR)] for part in (0, 1))
    score_rows(near_at, low, high, linked(range(near)))

    def soften(b, _):
        lanes = pl.ds(pl.multiple_of(b * BR, BR), BR)
        value = scores[:, lanes]
        powers = jnp.exp(value - jnp.max(value, axis=0, keepdims=True))
        total = jnp.sum(powers, axis=0, keepdims=True)
        weights[:, lanes] = (powers * (1.0 / total)).astype(jnp.bfloat16)
        return _

    lax.fori_loop(0, block_count, soften, 0)

    def scaled(block, at):
        return (block.astype(jnp.float32) * (1.0 / sum_recv[at][:1])).astype(jnp.bfloat16)

    def premix(stage, t):
        unit = labels[stage][t]
        for i in (0, 1):
            unit.cross(i).wait_recv()
            for part in (0, 1):
                block = unit.far_in[i, part]
                owns[t][part, :, rows + i * BR:rows + (i + 1) * BR] = scaled(block, i) if stage else block

        def body(c, _):
            lanes = lanes_of(c)
            for part in (0, 1):
                mix[part, bands[t], lanes] = jnp.dot(
                    owns[t][part], weights[:near_at, lanes], preferred_element_type=jnp.float32
                )
            return _

        lax.fori_loop(0, chunks, body, 0)

    def neighbour_mix(stage, t, finish):
        unit = labels[stage][t]
        gathered(unit)
        for k in range(near):
            for part, ref in ((0, unit.recv), (1, unit.fwd)):
                block = ref[places[part][k]]
                keys[t][part, :, k * BR:(k + 1) * BR] = scaled(block, sum_at[k]) if stage else block

        def body(c, _):
            lanes = lanes_of(c)
            total_sum = jnp.zeros((1, width), jnp.float32)
            for part in (0, 1):
                total = mix[part, bands[t], lanes] + jnp.dot(
                    keys[t][part], weights[near_at:, lanes], preferred_element_type=jnp.float32
                )
                mixed = MIXING * total + (1.0 - MIXING) * share[part, bands[t], lanes]
                squared = mixed * mixed
                total_sum += summed(squared, part, t)
                finish(c, lanes, part, squared)
            for b in range(in_chunk):
                value = jnp.broadcast_to(total_sum[:, b * BR:(b + 1) * BR], (8, BR))
                at = c * in_chunk + b
                sums[at] = value if t == 0 else sums[at] + value
            return _

        lax.fori_loop(0, chunks, body, 0)

    def middle(stage, t):
        def finish(c, lanes, part, squared):
            mix[part, bands[t], lanes] = squared
            put_blocks(stage + 1, part, t, c, squared.astype(jnp.bfloat16))

        return finish

    def last(t):
        def finish(c, lanes, part, squared):
            begin = pl.multiple_of(offsets[part] + bands[t].start, 8)
            out[pl.ds(begin, heights[t]), lanes] = squared

        return finish

    def sum_copy(s):
        return Copy(sum_send.at[s], sum_recv.at[s], sum_sem, (s,), everyone[s])

    def own_labels(c, _):
        lanes = lanes_of(c)
        parts = [sums[c * in_chunk + b][:1] for b in range(in_chunk)]
        scale = 1.0 / jnp.concatenate(parts, axis=1)
        for part in (0, 1):
            for t in (0, 1):
                owns[t][part, :, lanes] = (mix[part, bands[t], lanes] * scale).astype(jnp.bfloat16)
        return _

    for stage in range(ITERS):
        final = stage == ITERS - 1
        this = labels[stage]
        premix(stage, 0)
        pass_on(this[0], pure + RELAY)
        relay(this[1])
        neighbour_mix(stage, 0, last(0) if final else middle(stage, 0))
        if not final:
            later = labels[stage + 1]
            later[0].ex().start()
            side(later[0])
        premix(stage, 1)
        if not final:
            first(later[0])
        pass_on(this[1], pure + RELAY)
        neighbour_mix(stage, 1, last(1) if final else middle(stage, 1))
        if not final:
            for s in range(len(everyone)):
                sum_send[s] = sums[picks[s]]
                sum_copy(s).start()
            later[1].ex().start()
            side(later[1])
            relay(later[0])
            first(later[1])
            lax.fori_loop(0, chunks, own_labels, 0)
            for s in range(len(everyone)):
                sum_copy(s).wait_recv()

    for b in range(block_count):
        row_sums[:, b * BR:(b + 1) * BR] = sums[b]
    for copy in started.values():
        copy.wait_send()


def spread(cap, uneven, member_count, group_count, table, cross, emb, theirs, prior, links):
    block_count, _, features = emb.shape
    classes, rows = prior.shape
    half, heights = halves_of(classes)
    any_space = pl.BlockSpec(memory_space=pl.ANY)
    smem = pl.BlockSpec(memory_space=pltpu.SMEM)
    vmem = pl.BlockSpec(memory_space=pltpu.VMEM)
    bf16, f32 = jnp.bfloat16, jnp.float32
    keys = rows + 6 * BR
    partners = member_count + 1

    def unit(height, wide):
        counts = (
            (block_count,), (block_count,), (block_count,), (2 * cap,), (2 * cap + 1,), (2 * cap + 1,), (2,), (2, 2), (2, 2)
        )
        return [pltpu.VMEM(count + (height, wide), bf16) for count in counts]

    def dma(*shape):
        return pltpu.SemaphoreType.DMA((2,) + shape)

    units = 1 + 2 * ITERS
    return pl.pallas_call(
        functools.partial(spread_kernel, cap, uneven, member_count, group_count),
        out_shape=(pltpu.VMEM((classes, rows), f32), pltpu.VMEM((8, rows), f32)),
        in_specs=[smem] * 2 + [any_space] * 4,
        out_specs=(vmem, vmem),
        scratch_shapes=[
            pltpu.VMEM((2, half, rows), f32),
            pltpu.VMEM((links.shape[0], rows), jnp.int32),
            pltpu.VMEM((keys, rows), f32),
            pltpu.VMEM((keys, rows), bf16),
            pltpu.VMEM((2, half, rows), f32),
            pltpu.VMEM((block_count, 8, BR), f32),
            pltpu.VMEM((partners, 8, BR), f32),
            pltpu.VMEM((partners, 8, BR), f32),
            pltpu.VMEM((2, heights[0], rows + 2 * BR), bf16),
            pltpu.VMEM((2, heights[1], rows + 2 * BR), bf16),
            pltpu.VMEM((2, heights[0], 4 * BR), bf16),
            pltpu.VMEM((2, heights[1], 4 * BR), bf16),
            pltpu.VMEM((2, rows, features // 2), bf16),
            *unit(BR, features // 2),
            *(ref for _ in range(ITERS) for height in heights for ref in unit(height, BR)),
            pltpu.SemaphoreType.DMA((6,)),
            dma(units), dma(units, 2 * cap), dma(units, 2 * cap), dma(units, 2), dma(units, 2), dma(partners),
        ],
        compiler_params=pltpu.CompilerParams(
            collective_id=2 * cap - uneven, has_side_effects=True, vmem_limit_bytes=60 * 2**20
        ),
    )(table, cross, emb, theirs, prior, links)


def spread_body(embeddings, prior, source_member, source_block, cross_block, row_links):
    member_count = lax.axis_size("member")
    group_count = lax.axis_size("group")
    rows, features = embeddings.shape
    emb_blocks = embeddings.reshape(rows // BR, BR, features)
    table, theirs = route(source_member[0].T, source_block[0].T, emb_blocks, group_count)
    forms = ((6, True), (6, False), (7, True), (8, False))
    branches = [functools.partial(spread, cap, uneven, member_count, group_count) for cap, uneven in forms]
    squared, sums = lax.switch(
        jnp.clip(table[0] + 1 - 2 * forms[0][0], 0, len(forms) - 1), branches,
        table, cross_block[:, 0, :].T, emb_blocks, theirs, prior.T, row_links.T,
    )
    return (squared * (prior.shape[1] / sums[:1])).T


def solution(mesh):
    spread_fits = mesh.shape["member"] == 8
    body = spread_body if spread_fits else relay_body
    placed = (
        P(("group", "member"), None),
        P(("group", "member"), None),
        P("group", None, None),
        P("group", None, None),
        P(None, "member", None),
        P(("group", "member"), None),
    )
    return jax.shard_map(
        body, mesh=mesh, in_specs=placed, out_specs=P(("group", "member"), None), check_vma=False
    )
```
